32 devices in a mesh: grp: 2 (over x), seq: 8 (over z, y), head: 2 (over core).
Axes of the slice: x: 2, y: 2, z: 4, core: 2. Of those that a mesh axis runs over, the one named last changes fastest.
Arguments:
- queries: bfloat16 [8, 8, 40, 1024], P(('grp', 'head'), None, None, 'seq'), parts along dimension 0, may hold values from -160 to 160
- keys: bfloat16 [8, 8, 40, 1024], P('grp', None, None, 'seq'), parts along dimension 0, may hold values from -160 to 160
- values: bfloat16 [8, 8, 40, 1024], P('grp', None, None, 'seq'), parts along dimension 0, may hold values from -6 to 6
- final_gain: bfloat16 [1024], replicated, may hold values from 0.25 to 1.75
- out_weight: bfloat16 [1024, 64], replicated, may hold values from -0.1875 to 0.1875
- noisy_latent: bfloat16 [8, 16, 1280], P(('grp', 'head'), 'seq'), parts along dimension 0, may hold values from -6 to 6
- step_index: int32 [2], P('grp'), parts along dimension 0, may hold values from 0 to 15
- span_index: int32 [2], P('grp'), parts along dimension 0, may hold values from 0 to 63
- cache_flags: int32 [4, 2, 16], P('grp'), parts along dimension 0, may hold values 0 or 1
- latent_cache: bfloat16 [4, 2, 16, 1280], P('grp', 'head', 'seq'), parts along dimension 0, may hold values from -6 to 6
- feature_cache: bfloat16 [4, 2, 32, 61440], P('grp', 'head', 'seq'), parts along dimension 0, may hold values from -4 to 4
- first_weight: bfloat16 [432, 384], replicated, may hold values from -0.3125 to 0.3125
- first_gain: bfloat16 [384], replicated, may hold values from 0.25 to 1.75
- second_weight: bfloat16 [10368, 192], replicated, may hold values from -0.0625 to 0.0625
Outputs:
- clean_latent: bfloat16 [8, 16, 1280], P(('grp', 'head'), 'seq'), parts along dimension 0
- decoded: bfloat16 [8, 32, 30720], P(('grp', 'head'), 'seq'), parts along dimension 0
The draws below stay inside these ranges and needn't reach their ends.
There are 2 independent parts, one for each index of `grp`. The reference program is written for one: setup_inputs(seed, part) draws one part's arguments, and reference() takes and returns one part's arrays. A program takes and returns all parts, laid end to end along the dimension named above; an argument that names none is the same for every part. Nothing has to cross between parts.
All inputs are finite; a program needn't handle non-finite values.
Results may differ from the reference program's by a relative error of at most 0.013.
Values may be sent and summed in bfloat16 or wider, within the bound.
No kernel may reach another device: no remote copies, remote signals or barrier semaphores. Data moves between devices by JAX's collectives and lax.ppermute only.
A program may use at most 64 MiB of HBM per device.

```python
import jax
import jax.numpy as jnp
from jax import lax

HDIM = 128
CL = 16
C1 = 384
C2 = 192
F = 4
NSTEPS = 16
CSLOTS = 2
TW = 40
HEADS = 8
TR = 8
LR = 16
LW = 80
UR = 32
UW = 160


def attention_pair(key):
    token_count = F * TR * TW
    feature_count = HEADS * HDIM
    base_keys = jax.random.normal(jax.random.fold_in(key, 11), (token_count, feature_count), jnp.float32)
    base_queries = jax.random.normal(jax.random.fold_in(key, 12), (token_count, feature_count), jnp.float32)
    return (base_queries, base_keys)


def draw_queries(key, part):
    made_queries, made_keys = attention_pair(key)
    return jnp.clip(made_queries, -160.0, 160.0).reshape(F, TR, TW, HEADS * HDIM).astype(jnp.bfloat16)


def draw_keys(key, part):
    made_queries, made_keys = attention_pair(key)
    return jnp.clip(made_keys, -160.0, 160.0).reshape(F, TR, TW, HEADS * HDIM).astype(jnp.bfloat16)


def set_ends(values, stream_key, smallest, high):
    longest = values.shape.index(max(values.shape))
    spots = []
    for shift in (0, 1):
        where = [jax.random.randint(jax.random.fold_in(stream_key, axis), (), 0, length) for axis, length in enumerate(values.shape)]
        where[longest] = (where[longest] + shift) % values.shape[longest]
        spots.append(tuple(where))
    return values.at[spots[0]].set(smallest).at[spots[1]].set(high)


def block_levels(key, dims, cuts, low, top_value):
    def one(position, blocks):
        heights = jax.random.uniform(jax.random.fold_in(jax.random.fold_in(key, 6), position), (blocks,), jnp.float32, low / len(cuts), top_value / len(cuts))
        return jnp.repeat(jnp.exp(heights), dims[position] // blocks).reshape((-1,) + (1,) * (len(dims) - position - 1))

    level = one(*cuts[0])
    for cut in cuts[1:]:
        level = level * one(*cut)
    return level


def centred(own_key, dims, width, bound, split=(), kind=jnp.bfloat16):
    factor_of = block_levels(own_key, dims, split, -0.22, 0.18) if split else 1.0
    values = jax.random.normal(own_key, dims, jnp.float32) * width * factor_of
    return jnp.minimum(jnp.maximum(values, -bound), bound).astype(kind)


def setup_inputs(seed: int = 0, part: int = 0) -> dict:
    arg_keys = jax.random.split(jax.random.key(seed), 15)
    part_keys = jax.random.split(jax.random.fold_in(arg_keys[14], part), 15)
    return {
        "queries": draw_queries(jax.random.fold_in(jax.random.fold_in(arg_keys[14], part), 71), part),
        "keys": draw_keys(jax.random.fold_in(jax.random.fold_in(arg_keys[14], part), 71), part),
        "values": centred(part_keys[2], (F, TR, TW, HEADS * HDIM), 1.0, 6.0, ((3, 8),)),
        "final_gain": jnp.clip(1.0 + 0.15 * jax.random.normal(arg_keys[3], (HEADS * HDIM,), jnp.float32), 0.25, 1.75).astype(jnp.bfloat16),
        "out_weight": centred(arg_keys[4], (HEADS * HDIM, 4 * CL), (HEADS * HDIM) ** -0.5, 0.1875),
        "noisy_latent": centred(part_keys[5], (F, LR, LW * CL), 1.0, 6.0, ((0, 2), (1, 8))),
        "step_index": jax.random.randint(part_keys[6], (1,), 0, NSTEPS).astype(jnp.int32),
        "span_index": jax.random.randint(part_keys[7], (1,), 0, 64).astype(jnp.int32),
        "cache_flags": set_ends((jax.random.randint(part_keys[8], (CSLOTS, 2, LR), 0, 4) < 3).astype(jnp.int32), jax.random.fold_in(part_keys[8], 1), 0, 1),
        "latent_cache": centred(part_keys[9], (CSLOTS, 2, LR, LW * CL), 1.0, 6.0, ((1, 2), (2, 8))),
        "feature_cache": centred(part_keys[10], (CSLOTS, 2, UR, UW * C1), 0.6, 4.0, ((1, 2), (2, 8))),
        "first_weight": centred(arg_keys[11], (27 * CL, C1), (27 * CL) ** -0.5, 0.3125),
        "first_gain": jnp.clip(1.0 + 0.15 * jax.random.normal(arg_keys[12], (C1,), jnp.float32), 0.25, 1.75).astype(jnp.bfloat16),
        "second_weight": centred(arg_keys[13], (27 * C1, C2), (27 * C1) ** -0.5, 0.0625),
    }


SHIFT_FACTOR = 5.0
NORM_EPSILON = 1e-06

def noise_level_of(step_index):
    fraction = 1.0 - step_index[0].astype(jnp.float32) / NSTEPS
    return SHIFT_FACTOR * fraction / (1.0 + (SHIFT_FACTOR - 1.0) * fraction)

def attend(query_rows, key_rows, value_rows):
    scale = 1.0 / key_rows.shape[-1] ** 0.5
    scores = jnp.dot(query_rows, key_rows.T, preferred_element_type=jnp.float32) * scale
    row_max = lax.optimization_barrier(jnp.max(scores, axis=1, keepdims=True))
    exponent = jnp.exp(scores - row_max)
    accumulated = lax.optimization_barrier(jnp.sum(exponent, axis=1, keepdims=True))
    weights = exponent.astype(jnp.bfloat16)
    blended = jnp.dot(weights, value_rows, preferred_element_type=jnp.float32)
    return (blended / accumulated).astype(jnp.bfloat16)

def velocity_of(attended, final_gain, out_weight):
    features = attended.astype(jnp.float32)
    mean_square = lax.optimization_barrier(jnp.mean(features * features, axis=-1, keepdims=True))
    normed = features * lax.rsqrt(mean_square + NORM_EPSILON) * final_gain.astype(jnp.float32)
    return jnp.dot(normed, out_weight.astype(jnp.float32), precision=lax.Precision.HIGHEST)

def unpatch(patch_velocity):
    frame_count, row_count, col_count, patch_width = patch_velocity.shape
    channels = patch_width // 4
    grouped = patch_velocity.reshape(frame_count, row_count, col_count, 2, 2, channels)
    grouped = grouped.transpose(0, 1, 3, 2, 4, 5)
    return grouped.reshape(frame_count, 2 * row_count, 2 * col_count * channels)

def first_conv(extended, weight):
    channels = weight.shape[0] // 27
    frame_count = extended.shape[0] - 2
    row_count = extended.shape[1] - 2
    lattice = extended.reshape(frame_count + 2, row_count + 2, -1, channels)
    lattice = jnp.pad(lattice, ((0, 0), (0, 0), (1, 1), (0, 0)))
    col_count = lattice.shape[2] - 2
    shifted_taps = [lattice[step_t:step_t + frame_count, step_h:step_h + row_count, step_w:step_w + col_count] for step_t in range(3) for step_h in range(3) for step_w in range(3)]
    return jnp.dot(jnp.concatenate(shifted_taps, -1), weight, preferred_element_type=jnp.float32)

def activate(first_feat, first_gain):
    mean_square = lax.optimization_barrier(jnp.mean(first_feat * first_feat, axis=-1, keepdims=True))
    normed = first_feat * lax.rsqrt(mean_square + NORM_EPSILON) * first_gain.astype(jnp.float32)
    return jax.nn.silu(normed).astype(jnp.bfloat16)

def upsample(activated):
    return jnp.repeat(jnp.repeat(activated, 2, axis=1), 2, axis=2)

def second_conv(lattice, weight):
    channels = lattice.shape[3]
    frame_count = lattice.shape[0] - 2
    row_count = lattice.shape[1] - 2
    col_count = lattice.shape[2] - 2
    accumulated = None
    for step_t in range(3):
        for step_h in range(3):
            layer_slab = lattice[step_t:step_t + frame_count, step_h:step_h + row_count]
            stacked = jnp.concatenate([layer_slab[:, :, step_w:step_w + col_count] for step_w in range(3)], -1)
            first_row = (step_t * 3 + step_h) * 3 * channels
            weight_block = weight[first_row:first_row + 3 * channels]
            contribution = jnp.dot(stacked, weight_block, preferred_element_type=jnp.float32)
            accumulated = contribution if accumulated is None else accumulated + contribution
    return accumulated

def reference(queries, keys, values, final_gain, out_weight, noisy_latent, step_index, span_index, cache_flags, latent_cache, feature_cache, first_weight, first_gain, second_weight):
    frame_count, row_count, col_count, feature_count = queries.shape
    token_count = frame_count * row_count * col_count
    head_count = feature_count // HDIM

    def by_head(array):
        return array.reshape(token_count, head_count, HDIM).transpose(1, 0, 2)

    def attend_head(triple):
        return attend(triple[0], triple[1], triple[2])
    per_head = lax.map(attend_head, (by_head(queries), by_head(keys), by_head(values)))
    attended = per_head.transpose(1, 0, 2).reshape(frame_count, row_count, col_count, feature_count)
    velocity = unpatch(velocity_of(attended, final_gain, out_weight))
    clean_latent = (noisy_latent.astype(jnp.float32) - noise_level_of(step_index) * velocity).astype(jnp.bfloat16)
    cache_slot = (span_index[0] % CSLOTS).astype(jnp.int32)
    flags_now = lax.dynamic_index_in_dim(cache_flags, cache_slot, 0, keepdims=False).astype(jnp.bfloat16)
    prior_latent = lax.dynamic_index_in_dim(latent_cache, cache_slot, 0, keepdims=False) * flags_now[:, :, None]
    extended = jnp.concatenate([prior_latent, clean_latent], 0)
    extended = jnp.pad(extended, ((0, 0), (1, 1), (0, 0)))
    activated = activate(first_conv(extended, first_weight), first_gain)
    upsampled = upsample(activated)
    fine_flags = jnp.repeat(flags_now, 2, axis=1)
    prior_feature = lax.dynamic_index_in_dim(feature_cache, cache_slot, 0, keepdims=False)
    prior_feature = prior_feature.reshape(2, upsampled.shape[1], upsampled.shape[2], -1) * fine_flags[:, :, None, None]
    lattice = jnp.concatenate([prior_feature, upsampled], 0)
    lattice = jnp.pad(lattice, ((0, 0), (1, 1), (1, 1), (0, 0)))
    decoded = jnp.concatenate([second_conv(lattice[frame_index:frame_index + 3], second_weight) for frame_index in range(frame_count)], 0)
    return (clean_latent, decoded.astype(jnp.bfloat16).reshape(frame_count, upsampled.shape[1], -1))
```

```python
import jax
import jax.numpy as jnp
from jax import lax
from jax.experimental import pallas as pl
from jax.experimental.pallas import tpu as pltpu
from jax.sharding import PartitionSpec as P

NSTEPS = 16
CSLOTS = 2
SHIFT_FACTOR = 5.0
NORM_EPSILON = 1e-06
BF = jnp.bfloat16
F32 = jnp.float32
VMEM_LIMIT = 56 << 20


def params(dims=0):
    semantics = ("arbitrary",) * dims if dims else None
    return pltpu.CompilerParams(dimension_semantics=semantics, vmem_limit_bytes=VMEM_LIMIT)


def dot(left, right):
    return jnp.dot(left, right, preferred_element_type=F32)


def whole():
    return pl.BlockSpec(memory_space=pltpu.VMEM)


def smem():
    return pl.BlockSpec(memory_space=pltpu.SMEM)


def attention_kernel(q_ref, k_ref, v_ref, gain_ref, weight_ref, out_ref, *, cols, rows_total):
    frames, block, head_size = q_ref.shape
    rows = block // cols
    step = pl.program_id(0)
    if rows_total == rows:
        first = 0
    else:
        first = step * rows
    scale = 1.4426950408889634 / head_size**0.5
    keys = k_ref[...]
    values = jnp.concatenate([v_ref[...], jnp.ones_like(v_ref[...])], axis=1)
    gain = gain_ref[...].astype(F32)
    weight = weight_ref[...].astype(F32)
    none = jnp.zeros_like(weight)
    chosen = lax.broadcasted_iota(jnp.int32, (8, head_size), 0)
    total = None
    squares = []
    for f in range(frames):
        scores = lax.dot_general(
            q_ref[f], keys, (((1,), (1,)), ((), ())), preferred_element_type=F32
        )
        row_max = jnp.max(scores, axis=1, keepdims=True)
        weights = jnp.exp2((scores - row_max) * scale).astype(BF)
        blended = dot(weights, values)
        attended = (blended[:, :head_size] / blended[:, head_size:]).astype(BF).astype(F32)
        side = [none] * frames
        side[f] = weight
        wide = jnp.concatenate(side, axis=1).astype(BF)
        part = dot((attended * gain).astype(BF), wide)
        total = part if total is None else total + part
        squares.append(attended * attended)

    @pl.when(step == 0)
    def _():
        out_ref[0, 0] = jnp.zeros(out_ref.shape[2:], BF)
        out_ref[rows_total - 1, 2] = jnp.zeros(out_ref.shape[2:], BF)

    for r in range(rows):
        sums = None
        for f in range(frames):
            piece = squares[f][r * cols : (r + 1) * cols].astype(BF)
            line = lax.dot_general(
                (chosen == f).astype(F32).astype(BF),
                piece,
                (((1,), (1,)), ((), ())),
                preferred_element_type=F32,
            )
            sums = line if sums is None else sums + line
        lanes = total.shape[1]
        sums = jnp.concatenate([sums, jnp.zeros((8, lanes - cols), F32)], axis=1)
        unit = jnp.concatenate([total[r * cols : (r + 1) * cols], sums], axis=0).astype(BF)
        row = first + r
        out_ref[row, 1] = unit

        @pl.when(row + 1 < rows_total)
        def _():
            out_ref[jnp.minimum(row + 1, rows_total - 1), 0] = unit

        @pl.when(row > 0)
        def _():
            out_ref[jnp.maximum(row - 1, 0), 2] = unit


def attention(queries, keys, values, final_gain, out_weight, slab):
    frames, rows_total, cols, head_size = queries.shape
    q = queries.reshape(frames, rows_total * cols, head_size)
    k = keys.reshape(-1, head_size)
    v = values.reshape(-1, head_size)
    rows = 4 if rows_total % 4 == 0 else rows_total
    width = out_weight.shape[1]
    lanes = frames * width
    unit = cols + 8

    def kernel(slab_ref, *refs):
        attention_kernel(*refs, cols=cols, rows_total=rows_total)

    grid_spec = pltpu.PrefetchScalarGridSpec(
        num_scalar_prefetch=1,
        grid=(rows_total // rows,),
        in_specs=[
            pl.BlockSpec((frames, rows * cols, head_size), lambda i, s: (0, i, 0)),
            pl.BlockSpec(k.shape, lambda i, s: (0, 0)),
            pl.BlockSpec(v.shape, lambda i, s: (0, 0)),
            pl.BlockSpec((1, head_size), lambda i, s: (0, s[0])),
            pl.BlockSpec((head_size, width), lambda i, s: (s[0], 0)),
        ],
        out_specs=pl.BlockSpec((rows_total, 3, unit, lanes), lambda i, s: (0, 0, 0, 0)),
    )
    count = frames * rows_total * cols
    return pl.pallas_call(
        kernel,
        grid_spec=grid_spec,
        out_shape=jax.ShapeDtypeStruct((rows_total, 3, unit, lanes), BF),
        compiler_params=params(1),
        cost_estimate=pl.CostEstimate(
            flops=6 * count * k.shape[0] * head_size,
            bytes_accessed=2 * (q.size + k.size + v.size),
            transcendentals=count * k.shape[0],
        ),
        name="attention",
    )(slab, q, k, v, final_gain.reshape(1, -1), out_weight)


def prepare_kernel(span_ref, place_ref, flags_ref, cache_ref, small_ref, own_ref, up_ref, down_ref, scr):
    tiles, rows, lanes = cache_ref.shape[1:]
    cols, channels = own_ref.shape[2:]
    pieces = channels // lanes
    slot = lax.rem(span_ref[0], CSLOTS)
    coarse = rows // 2
    flags = [
        flags_ref[slot, place_ref[1], place_ref[0] * coarse + r].astype(F32) for r in range(coarse)
    ]

    def unpack(i, carry):
        for n in range(16):
            at = i * 16 + n
            scr[pl.ds(pl.multiple_of(at * rows, rows), rows), :] = cache_ref[0, at].astype(F32)
        return carry

    lax.fori_loop(0, tiles // 16, unpack, 0)
    for r in range(rows):
        for b in range(2):
            for q in range(pieces):
                start = (b * pieces + q) * rows + r
                piece = scr[pl.ds(start, cols, stride=2 * pieces * rows), :]
                piece = (piece * flags[r // 2]).astype(BF)
                own_ref[r, b, :, q * lanes : (q + 1) * lanes] = piece
                if r == 0:
                    up_ref[b * cols : (b + 1) * cols, q * lanes : (q + 1) * lanes] = piece
                if r == rows - 1:
                    down_ref[b * cols : (b + 1) * cols, q * lanes : (q + 1) * lanes] = piece
    extra = small_ref[...]
    up_ref[2 * cols :, :] = extra
    down_ref[2 * cols :, :] = extra


def prepare(span_index, place, cache_flags, feature_cache, small, channels):
    slots, _, rows, width = feature_cache.shape
    tiles = width // 128
    view = feature_cache.reshape(slots, rows, tiles, 128).transpose(0, 2, 1, 3)
    cols = width // channels // 2
    halo = 2 * cols + small.shape[0]
    grid_spec = pltpu.PrefetchScalarGridSpec(
        num_scalar_prefetch=3,
        grid=(1,),
        in_specs=[
            pl.BlockSpec((1, tiles, rows, 128), lambda i, s, p, f: (lax.rem(s[0], CSLOTS), 0, 0, 0)),
            pl.BlockSpec(small.shape, lambda i, s, p, f: (0, 0)),
        ],
        out_specs=[
            pl.BlockSpec((rows, 2, cols, channels), lambda i, s, p, f: (0, 0, 0, 0)),
            pl.BlockSpec((halo, channels), lambda i, s, p, f: (0, 0)),
            pl.BlockSpec((halo, channels), lambda i, s, p, f: (0, 0)),
        ],
        scratch_shapes=[pltpu.VMEM((tiles * rows, 128), F32)],
    )
    return pl.pallas_call(
        prepare_kernel,
        grid_spec=grid_spec,
        out_shape=[
            jax.ShapeDtypeStruct((rows, 2, cols, channels), BF),
            jax.ShapeDtypeStruct((halo, channels), BF),
            jax.ShapeDtypeStruct((halo, channels), BF),
        ],
        compiler_params=params(1),
        cost_estimate=pl.CostEstimate(
            flops=rows * width, bytes_accessed=6 * rows * width, transcendentals=0
        ),
        name="prepare",
    )(span_index, place, cache_flags, view, small)


def shift_down(array):
    moved = pltpu.roll(array, 1, axis=0)
    rows = lax.broadcasted_iota(jnp.int32, array.shape, 0)
    return jnp.where(rows == 0, 0.0, moved)


def shift_up(array):
    count = array.shape[0]
    moved = pltpu.roll(array, count - 1, axis=0)
    rows = lax.broadcasted_iota(jnp.int32, array.shape, 0)
    return jnp.where(rows == count - 1, 0.0, moved)


def cached_kernel(place_ref, own_ref, above_ref, below_ref, weight_ref, out_ref, var):
    rows, _, cols, channels = own_ref.shape
    for r in range(rows + 2):
        if r == 0:
            even, odd = above_ref[:cols], above_ref[cols : 2 * cols]
        elif r == rows + 1:
            even, odd = below_ref[:cols], below_ref[cols : 2 * cols]
        else:
            even, odd = own_ref[r - 1, 0], own_ref[r - 1, 1]
        var[0, r] = shift_down(odd.astype(F32)).astype(BF)
        var[1, r] = even
        var[2, r] = odd
        var[3, r] = shift_up(even.astype(F32)).astype(BF)

    def contribution(base):
        sides = []
        for b in range(2):
            total = None
            for h in range(3):
                left = jnp.concatenate(
                    [
                        var[b + w, h : h + rows].reshape(rows * cols, channels)
                        for w in range(3)
                    ],
                    axis=1,
                )
                start = pl.multiple_of(base + h * 3 * channels, channels)
                part = dot(left, weight_ref[pl.ds(start, 3 * channels), :])
                total = part if total is None else total + part
            sides.append(total)
        return jnp.concatenate(sides, axis=1)

    head = place_ref[1]
    first = contribution(head * (9 * channels))
    out_ref[0] = first.astype(BF).reshape(out_ref.shape[1:])

    @pl.when(head == 0)
    def _():
        out_ref[1] = jnp.zeros(out_ref.shape[1:], BF)

    @pl.when(head != 0)
    def _():
        out_ref[1] = contribution(0).astype(BF).reshape(out_ref.shape[1:])


def cached(place, own, above, below, weight):
    rows, _, cols, channels = own.shape
    return pl.pallas_call(
        cached_kernel,
        in_specs=[smem(), whole(), whole(), whole(), whole()],
        out_specs=whole(),
        out_shape=jax.ShapeDtypeStruct((2, rows, cols, 2 * weight.shape[1]), BF),
        scratch_shapes=[pltpu.VMEM((4, rows + 2, cols, channels), BF)],
        compiler_params=params(),
        cost_estimate=pl.CostEstimate(
            flops=2 * 2 * rows * 2 * cols * 9 * channels * weight.shape[1],
            bytes_accessed=2 * (own.size + weight.size),
            transcendentals=0,
        ),
        name="cached",
    )(place, own, above, below, weight)


def spread(source_ref, var):
    frames, coarse = source_ref.shape[:2]
    for f in range(frames):
        for r in range(coarse):
            plain = source_ref[f, r]
            wide = plain.astype(F32)
            var[0, f, r] = shift_down(wide).astype(BF)
            var[1, f, r] = plain
            var[2, f, r] = shift_up(wide).astype(BF)


def upsampled_part(var, weight_ref, frame, step_t, b):
    coarse, cols, channels = var.shape[2:]
    fine = 2 * (coarse - 2)
    total = None
    for h in range(3):
        lines = []
        for row in range(fine):
            at = (row + h - 1) // 2 + 1
            lines.append(
                jnp.concatenate(
                    [var[(b + w + 1) // 2, frame, at] for w in range(3)], axis=1
                )
            )
        start = (step_t * 3 + h) * 3 * channels
        part = dot(jnp.concatenate(lines, axis=0), weight_ref[start : start + 3 * channels, :])
        total = part if total is None else total + part
    return total


def own_kernel(source_ref, weight_ref, out_ref, var):
    spread(source_ref, var)
    width = weight_ref.shape[1]
    for f, pairs in ((0, ((0, 2),)), (1, ((0, 1), (1, 2)))):
        sides = []
        for b in range(2):
            total = None
            for frame, step_t in pairs:
                part = upsampled_part(var, weight_ref, frame, step_t, b)
                total = part if total is None else total + part
            sides.append(total)
        out_ref[f] = jnp.concatenate(sides, axis=1).reshape(out_ref.shape[1:])


def own_part(activated, weight):
    frames, coarse, cols, channels = activated.shape
    fine = 2 * (coarse - 2)
    return pl.pallas_call(
        own_kernel,
        in_specs=[whole(), whole()],
        out_specs=whole(),
        out_shape=jax.ShapeDtypeStruct((frames, fine, cols, 2 * weight.shape[1]), F32),
        scratch_shapes=[pltpu.VMEM((3, frames, coarse, cols, channels), BF)],
        compiler_params=params(),
        cost_estimate=pl.CostEstimate(
            flops=3 * 2 * fine * 2 * cols * 9 * channels * weight.shape[1],
            bytes_accessed=2 * (activated.size + weight.size),
            transcendentals=0,
        ),
        name="own_part",
    )(activated, weight)


def prior_kernel(place_ref, source_ref, cached_ref, own_ref, weight_ref, out_ref, var, total_ref, scr):
    frames, fine, cols, width = own_ref.shape
    head = place_ref[1]

    @pl.when(head == 0)
    def _():
        total_ref[...] = own_ref[...] + (
            cached_ref[...].astype(F32) + source_ref[...].astype(F32)
        )

    @pl.when(head != 0)
    def _():
        spread(source_ref, var)
        for f, pairs in ((0, ((0, 0), (1, 1))), (1, ((1, 0),))):
            sides = []
            for b in range(2):
                total = None
                for frame, step_t in pairs:
                    part = upsampled_part(var, weight_ref, frame, step_t, b)
                    total = part if total is None else total + part
                sides.append(total)
            both = jnp.concatenate(sides, axis=1).reshape(fine, cols, width)
            total_ref[f] = own_ref[f] + both

    pieces = width // 128
    for f in range(frames):
        for row in range(fine):
            for q in range(pieces):
                scr[pl.ds(q * fine + row, cols, stride=pieces * fine), :] = total_ref[
                    f, row, :, q * 128 : (q + 1) * 128
                ]

        def pack(i, carry):
            for n in range(16):
                at = i * 16 + n
                out_ref[f, at] = scr[pl.ds(pl.multiple_of(at * fine, fine), fine), :].astype(BF)
            return carry

        lax.fori_loop(0, out_ref.shape[1] // 16, pack, 0)


def prior_part(place, received, cached_sum, own_sum, weight):
    frames, coarse, cols, channels = received.shape
    _, fine, _, width = own_sum.shape
    tiles = cols * width // 128
    out = pl.pallas_call(
        prior_kernel,
        in_specs=[smem(), whole(), whole(), whole(), whole()],
        out_specs=whole(),
        out_shape=jax.ShapeDtypeStruct((frames, tiles, fine, 128), BF),
        scratch_shapes=[
            pltpu.VMEM((3, frames, coarse, cols, channels), BF),
            pltpu.VMEM(own_sum.shape, F32),
            pltpu.VMEM((tiles * fine, 128), F32),
        ],
        compiler_params=params(),
        cost_estimate=pl.CostEstimate(
            flops=3 * 2 * fine * 2 * cols * 9 * channels * weight.shape[1],
            bytes_accessed=2 * (received.size + weight.size),
            transcendentals=0,
        ),
        name="prior_part",
    )(place, received, cached_sum, own_sum, weight)
    return out.transpose(0, 2, 1, 3).reshape(frames, fine, cols * width)


def latent_kernel(step_ref, place_ref, parts_ref, own_ref, above_ref, below_ref, clean_ref, send_ref):
    sources, three, unit, lanes = parts_ref.shape
    cols = own_ref.shape[0]
    features = sources * 128
    fraction = 1.0 - step_ref[0].astype(F32) / NSTEPS
    fraction = jnp.full((1, lanes), fraction, F32)
    level = SHIFT_FACTOR * fraction / (1.0 + (SHIFT_FACTOR - 1.0) * fraction)
    total = parts_ref[0].astype(F32)
    for source in range(1, sources):
        total = total + parts_ref[source].astype(F32)
    half = lax.broadcasted_iota(jnp.int32, (cols, lanes), 1) < lanes // 2
    first_group = place_ref[1] == 0
    for k, small_ref in ((0, above_ref), (1, own_ref), (2, below_ref)):
        small = small_ref[...] if k == 1 else small_ref[small_ref.shape[0] - cols :]
        sums = jnp.transpose(total[k, cols:unit])[:cols]
        scale = lax.rsqrt(sums / features + NORM_EPSILON)
        scale = jnp.where(half, scale[:, 0:1], scale[:, 1:2])
        velocity = total[k, :cols] * scale
        clean = (small[:, :lanes].astype(F32) - level * velocity).astype(BF)
        clean_ref[k] = clean

        @pl.when(first_group)
        def _():
            send_ref[k] = clean

        @pl.when(jnp.logical_not(first_group))
        def _():
            send_ref[k] = small[:, lanes : 2 * lanes]


def latent(step_index, place, parts, own, above, below):
    sources, three, unit, lanes = parts.shape
    cols = own.shape[0]
    shape = jax.ShapeDtypeStruct((three, cols, lanes), BF)
    return pl.pallas_call(
        latent_kernel,
        in_specs=[smem(), smem(), whole(), whole(), whole(), whole()],
        out_specs=[whole(), whole()],
        out_shape=[shape, shape],
        compiler_params=params(),
        cost_estimate=pl.CostEstimate(
            flops=2 * parts.size, bytes_accessed=2 * parts.size, transcendentals=0
        ),
        name="latent",
    )(step_index, place, parts, own, above, below)


def first_kernel(
    place_ref, clean_ref, received_ref, own_ref, above_ref, below_ref, weight_ref, gain_ref, cached_ref, act_ref, send_ref, left, scr
):
    three, cols, lanes = clean_ref.shape
    frames, coarse = act_ref.shape[:2]
    channels = act_ref.shape[3]
    group = lanes // 4
    slot = lanes // 2
    part = group // 2
    head = place_ref[1]
    cached_old = jnp.concatenate(
        [
            above_ref[above_ref.shape[0] - cols :, lanes : 2 * lanes].astype(F32),
            own_ref[:, lanes : 2 * lanes].astype(F32),
            below_ref[below_ref.shape[0] - cols :, lanes : 2 * lanes].astype(F32),
        ],
        axis=0,
    )
    clean = jnp.concatenate([clean_ref[k].astype(F32) for k in range(three)], axis=0)
    arrived = jnp.concatenate([received_ref[k].astype(F32) for k in range(three)], axis=0)
    lane = lax.broadcasted_iota(jnp.int32, clean.shape, 1)
    line = lax.broadcasted_iota(jnp.int32, clean.shape, 0)
    at = lax.rem(line, cols)
    older = jnp.where(
        head == 0, jnp.where(lane < lanes // 2, cached_old, arrived), arrived
    )
    pieces = {}
    for source, x in enumerate((older, clean)):
        height = x.shape[0]
        before = jnp.where(at == 0, 0.0, pltpu.roll(x, 1, axis=0))
        after = jnp.where(at == cols - 1, 0.0, pltpu.roll(x, height - 1, axis=0))
        for f in range(2):
            for a in range(2):
                off = f * (lanes // 2) + a * group
                for side in range(2):
                    base = side * slot

                    def moved(array, shift):
                        shift = shift % lanes
                        return pltpu.roll(array, shift, axis=1) if shift else array

                    low = lane - base
                    even = jnp.where(
                        (low >= 0) & (low < part),
                        moved(before, base - off - part),
                        jnp.where(
                            (low >= part) & (low < 3 * part), moved(x, base + part - off), 0.0
                        ),
                    )
                    odd = jnp.where(
                        (low >= 0) & (low < 2 * part),
                        moved(x, base - off),
                        jnp.where(
                            (low >= 2 * part) & (low < 3 * part),
                            moved(after, base + 2 * part - off),
                            0.0,
                        ),
                    )
                    pieces[source * 2 + f, a, side, 0] = even
                    pieces[source * 2 + f, a, side, 1] = odd

    def piece(p, fo, ro, n):
        frame = fo + n // 3
        row = ro + n % 3
        k = row // 2
        return pieces[frame, row % 2, n % 2, p][k * cols : (k + 1) * cols]

    for p in range(2):
        for fo in range(frames):
            for ro in range(coarse):
                start = ((p * frames + fo) * coarse + ro) * cols
                for j in range(5):
                    block = piece(p, fo, ro, 2 * j)
                    if 2 * j + 1 < 9:
                        block = block + piece(p, fo, ro, 2 * j + 1)
                    left[start : start + cols, j * lanes : (j + 1) * lanes] = block.astype(BF)

    feat = dot(left[...], weight_ref[...])
    mean_square = jnp.mean(feat * feat, axis=-1, keepdims=True)
    normed = feat * lax.rsqrt(mean_square + NORM_EPSILON) * gain_ref[...].astype(F32)
    active = normed / (1.0 + jnp.exp(-normed))
    slab = place_ref[0]
    last = place_ref[2] - 1
    keep_first = jnp.where(slab == 0, 0.0, 1.0)
    keep_last = jnp.where(slab == last, 0.0, 1.0)
    for p in range(2):
        for fo in range(frames):
            for ro in range(coarse):
                start = ((p * frames + fo) * coarse + ro) * cols
                block = active[start : start + cols]
                if ro == 0:
                    block = block * keep_first
                if ro == coarse - 1:
                    block = block * keep_last
                to = (fo * coarse + ro) * 2 * cols + p
                for q in range(channels // 128):
                    scr[q, pl.ds(to, cols, stride=2), :] = block[:, q * 128 : (q + 1) * 128]
    for fo in range(frames):
        for ro in range(coarse):
            to = (fo * coarse + ro) * 2 * cols
            for q in range(channels // 128):
                act_ref[fo, ro, :, q * 128 : (q + 1) * 128] = scr[q, to : to + 2 * cols, :].astype(BF)

    @pl.when(head == 0)
    def _():
        send_ref[...] = act_ref[...]

    @pl.when(head != 0)
    def _():
        send_ref[...] = cached_ref[...]


def first(place, clean, received, own, above, below, weight, gain, cached_sum):
    three, cols, lanes = clean.shape
    shape = jax.ShapeDtypeStruct(cached_sum.shape, BF)
    frames, coarse, wide, channels = cached_sum.shape
    height = frames * coarse * wide
    return pl.pallas_call(
        first_kernel,
        in_specs=[smem()] + [whole()] * 8,
        out_specs=[whole(), whole()],
        out_shape=[shape, shape],
        scratch_shapes=[
            pltpu.VMEM((height, 5 * lanes), BF),
            pltpu.VMEM((channels // 128, height, 128), F32),
        ],
        compiler_params=params(),
        cost_estimate=pl.CostEstimate(
            flops=2 * height * weight.size, bytes_accessed=4 * cached_sum.size, transcendentals=height * channels
        ),
        name="first",
    )(place, clean, received, own, above, below, weight, gain, cached_sum)


def swapped(array, axis):
    return lax.ppermute(array, axis, [(0, 1), (1, 0)])


def body(
    queries,
    keys,
    values,
    final_gain,
    out_weight,
    noisy_latent,
    step_index,
    span_index,
    cache_flags,
    latent_cache,
    feature_cache,
    first_weight,
    first_gain,
    second_weight,
):
    frames, token_rows, cols, head_size = queries.shape
    channels = first_weight.shape[1]
    width = first_weight.shape[0] // 27
    slab = lax.axis_index("seq")
    slabs = lax.axis_size("seq")
    head = lax.axis_index("head")
    place = jnp.stack([slab, head, jnp.int32(slabs)]).astype(jnp.int32)

    slot = span_index[0] % CSLOTS
    own_latent = lax.dynamic_index_in_dim(latent_cache, slot, 0, keepdims=False)[0]
    rows = own_latent.shape[0]
    flags = lax.dynamic_slice(cache_flags, (slot, head, slab * rows), (1, 1, rows))[0, 0]
    own_latent = own_latent * flags[:, None].astype(BF)
    noisy_tokens = noisy_latent.reshape(frames, 2, cols, 2 * width).transpose(2, 0, 1, 3)
    noisy_tokens = noisy_tokens.reshape(cols, frames * 4 * width)
    old_tokens = own_latent.reshape(2, cols, 2 * width).transpose(1, 0, 2).reshape(cols, 4 * width)
    small = jnp.concatenate([noisy_tokens, old_tokens, old_tokens, jnp.zeros((cols, channels - 16 * width), BF)], 1)

    own_frame, up, down = prepare(span_index, place, cache_flags, feature_cache, small, channels)
    above = lax.ppermute(down, "seq", [(i, i + 1) for i in range(slabs - 1)])
    below = lax.ppermute(up, "seq", [(i + 1, i) for i in range(slabs - 1)])

    sent = attention(queries, keys, values, final_gain, out_weight, slab.reshape(1).astype(jnp.int32))
    parts = lax.all_to_all(sent, "seq", 0, 0, tiled=True)
    cached_sum = cached(place, own_frame, above, below, second_weight)

    clean, send = latent(step_index, place, parts, small, above, below)
    received = swapped(send, "head")
    spare = 64 - 3 * width
    padded = jnp.pad(first_weight.reshape(9, 3 * width, channels), ((0, 1), (0, spare), (0, 0)))
    padded = padded.reshape(640, channels)
    activated, send = first(
        place, clean, received, small, above, below, padded, first_gain.reshape(1, -1), cached_sum
    )
    arrived = swapped(send, "head")
    own_sum = own_part(activated, second_weight)
    decoded = prior_part(place, arrived, cached_sum, own_sum, second_weight)

    tokens = clean[1].reshape(cols, frames, 2, 2 * width).transpose(1, 2, 0, 3)
    return (tokens.reshape(frames, 2, 2 * cols * width), decoded)


def solution(mesh):
    in_specs = (
        P(("grp", "head"), None, None, "seq"),
        P("grp", None, None, "seq"),
        P("grp", None, None, "seq"),
        P(),
        P(),
        P(("grp", "head"), "seq", None),
        P("grp"),
        P("grp"),
        P("grp", None, None),
        P("grp", "head", "seq", None),
        P("grp", "head", "seq", None),
        P(),
        P(),
        P(),
    )
    out_specs = (P(("grp", "head"), "seq", None), P(("grp", "head"), "seq", None))
    return jax.shard_map(body, mesh=mesh, in_specs=in_specs, out_specs=out_specs, check_vma=False)
```

```python
import jax
import jax.numpy as jnp
from jax import lax
from jax.experimental import pallas as pl
from jax.experimental.pallas import tpu as pltpu
from jax.sharding import PartitionSpec as P

NSTEPS = 16
CSLOTS = 2
SHIFT_FACTOR = 5.0
NORM_EPSILON = 1e-06
BF = jnp.bfloat16
F32 = jnp.float32
LAST = (((1,), (1,)), ((), ()))


def params(dims=0, mib=20):
    semantics = ("arbitrary",) * dims if dims else None
    return pltpu.CompilerParams(dimension_semantics=semantics, vmem_limit_bytes=mib << 20)


def dot(left, right):
    return jnp.dot(left, right, preferred_element_type=F32)


def dot_last(left, right):
    return lax.dot_general(left, right, LAST, preferred_element_type=F32)


def whole():
    return pl.BlockSpec(memory_space=pltpu.VMEM)


def smem():
    return pl.BlockSpec(memory_space=pltpu.SMEM)


def attention_kernel(q_ref, k_ref, v_ref, gain_ref, weight_ref, out_ref, *, cols, rows_total):
    frames, block, head_size = q_ref.shape
    rows = block // cols
    step = pl.program_id(0)
    slab = lax.axis_index("seq")
    scale = 1.4426950408889634 / head_size**0.5
    keys = k_ref[...]
    values = jnp.concatenate([v_ref[...], jnp.ones_like(v_ref[...])], axis=1)
    gains = gain_ref[...].astype(F32)
    chosen = lax.broadcasted_iota(jnp.int32, gains.shape, 0) == slab
    gain = jnp.sum(jnp.where(chosen, gains, 0.0), axis=0, keepdims=True)
    start = pl.multiple_of(slab * head_size, head_size)
    weight = weight_ref[:, pl.ds(start, head_size)]
    none = jnp.zeros_like(weight)
    line_of = lax.broadcasted_iota(jnp.int32, (8, head_size), 0)
    total = None
    squares = []
    for f in range(frames):
        scores = dot_last(q_ref[f], keys)
        row_max = jnp.max(scores, axis=1, keepdims=True)
        weights = jnp.exp2((scores - row_max) * scale).astype(BF)
        blended = dot(weights, values)
        attended = (blended[:, :head_size] / blended[:, head_size:]).astype(BF).astype(F32)
        side = [none] * frames
        side[f] = weight
        part = dot_last((attended * gain).astype(BF), jnp.concatenate(side, axis=0))
        total = part if total is None else total + part
        squares.append(attended * attended)

    @pl.when(step == 0)
    def _():
        out_ref[0, 0] = jnp.zeros(out_ref.shape[2:], BF)
        out_ref[rows_total - 1, 2] = jnp.zeros(out_ref.shape[2:], BF)

    for r in range(rows):
        sums = None
        for f in range(frames):
            piece = squares[f][r * cols : (r + 1) * cols].astype(BF)
            line = dot_last((line_of == f).astype(F32).astype(BF), piece)
            sums = line if sums is None else sums + line
        lanes = total.shape[1]
        sums = jnp.concatenate([sums, jnp.zeros((8, lanes - cols), F32)], axis=1)
        unit = jnp.concatenate([total[r * cols : (r + 1) * cols], sums], axis=0).astype(BF)
        row = step * rows + r
        out_ref[row, 1] = unit

        @pl.when(row + 1 < rows_total)
        def _():
            out_ref[jnp.minimum(row + 1, rows_total - 1), 0] = unit

        @pl.when(row > 0)
        def _():
            out_ref[jnp.maximum(row - 1, 0), 2] = unit


def attention(queries, keys, values, final_gain, out_weight):
    frames, rows_total, cols, head_size = queries.shape
    q = queries.reshape(frames, rows_total * cols, head_size)
    k = keys.reshape(-1, head_size)
    v = values.reshape(-1, head_size)
    gains = final_gain.reshape(-1, head_size)
    weight = out_weight.T
    rows = 4 if rows_total % 4 == 0 else rows_total
    lanes = frames * weight.shape[0]
    unit = cols + 8

    def kernel(*refs):
        attention_kernel(*refs, cols=cols, rows_total=rows_total)

    count = frames * rows_total * cols
    return pl.pallas_call(
        kernel,
        grid=(rows_total // rows,),
        in_specs=[
            pl.BlockSpec((frames, rows * cols, head_size), lambda i: (0, i, 0)),
            pl.BlockSpec(k.shape, lambda i: (0, 0)),
            pl.BlockSpec(v.shape, lambda i: (0, 0)),
            pl.BlockSpec(gains.shape, lambda i: (0, 0)),
            pl.BlockSpec(weight.shape, lambda i: (0, 0)),
        ],
        out_specs=pl.BlockSpec((rows_total, 3, unit, lanes), lambda i: (0, 0, 0, 0)),
        out_shape=jax.ShapeDtypeStruct((rows_total, 3, unit, lanes), BF),
        compiler_params=params(1, 40),
        cost_estimate=pl.CostEstimate(
            flops=6 * count * k.shape[0] * head_size,
            bytes_accessed=2 * (q.size + k.size + v.size),
            transcendentals=count * k.shape[0],
        ),
        name="attention",
    )(q, k, v, gains, weight)


def lane_groups(array, group):
    return lax.broadcasted_iota(jnp.int32, array.shape, 1) // group


def moved(array, shift):
    lanes = array.shape[1]
    shift = shift % lanes
    return pltpu.roll(array, shift, axis=1) if shift else array


def prepare_kernel(
    span_ref, flags_ref, cache_ref, noisy_ref, latent_ref, own_ref, up_ref, down_ref, small_ref, scr, lat
):
    tiles, rows, lanes = cache_ref.shape[1:]
    cols, channels = own_ref.shape[2:]
    pieces = channels // lanes
    slot = lax.rem(span_ref[0], CSLOTS)
    slab = lax.axis_index("seq")
    head = lax.axis_index("head")
    coarse = rows // 2
    flags = [flags_ref[slot, head, slab * coarse + r].astype(F32) for r in range(coarse)]

    frames, chunks, halves = noisy_ref.shape[:3]
    groups = frames * halves
    group = lanes // groups
    for f in range(frames + 1):
        for i in range(chunks):
            tile = latent_ref[0, i] if f == frames else noisy_ref[f, i]
            lat[pl.ds((f * chunks + i) * halves, halves), :] = tile.astype(F32)
    lines = [
        [lat[pl.ds(f * chunks * halves + a, chunks, stride=halves), :] for a in range(halves)]
        for f in range(frames + 1)
    ]
    noisy = [lines[f][a] for f in range(frames) for a in range(halves)]
    old = [lines[frames][a] * flags[a] for f in range(frames) for a in range(halves)]
    base = (frames + 1) * chunks * halves
    tokens = chunks * groups
    for n, parts in enumerate((noisy, old)):
        at = base + n * tokens
        for m in range(groups):
            total = None
            for g, part in enumerate(parts):
                term = jnp.where(lane_groups(part, group) == g, moved(part, group * (g - m)), 0.0)
                total = term if total is None else total + term
            lat[pl.ds(at + m, chunks, stride=groups), :] = total
        block = lat[at : at + tokens, :].astype(BF)
        small_ref[:, n * lanes : (n + 1) * lanes] = block
        up_ref[2 * cols :, n * lanes : (n + 1) * lanes] = block
        down_ref[2 * cols :, n * lanes : (n + 1) * lanes] = block
    rest = jnp.zeros((tokens, channels - 2 * lanes), BF)
    up_ref[2 * cols :, 2 * lanes :] = rest
    down_ref[2 * cols :, 2 * lanes :] = rest

    def unpack(i, carry):
        for n in range(16):
            at = i * 16 + n
            scr[pl.ds(pl.multiple_of(at * rows, rows), rows), :] = cache_ref[0, at].astype(F32)
        return carry

    lax.fori_loop(0, tiles // 16, unpack, 0)
    for r in range(rows):
        for b in range(2):
            for q in range(pieces):
                start = (b * pieces + q) * rows + r
                piece = scr[pl.ds(start, cols, stride=2 * pieces * rows), :]
                piece = (piece * flags[r // 2]).astype(BF)
                own_ref[r, b, :, q * lanes : (q + 1) * lanes] = piece
                if r == 0:
                    up_ref[b * cols : (b + 1) * cols, q * lanes : (q + 1) * lanes] = piece
                if r == rows - 1:
                    down_ref[b * cols : (b + 1) * cols, q * lanes : (q + 1) * lanes] = piece


def tiled(array):
    *lead, rows, width = array.shape
    count = len(lead)
    view = array.reshape(*lead, rows, width // 128, 128)
    return view.transpose(*range(count), count + 1, count, count + 2)


def prepare(span_index, cache_flags, feature_cache, noisy_latent, latent_cache, channels):
    slots, _, rows, width = feature_cache.shape
    tiles = width // 128
    cols = width // channels // 2
    noisy = tiled(noisy_latent)
    frames, chunks, halves = noisy.shape[:3]
    tokens = chunks * frames * halves
    halo = 2 * cols + tokens
    grid_spec = pltpu.PrefetchScalarGridSpec(
        num_scalar_prefetch=2,
        grid=(1,),
        in_specs=[
            pl.BlockSpec((1, tiles, rows, 128), lambda i, s, f: (lax.rem(s[0], CSLOTS), 0, 0, 0)),
            pl.BlockSpec(noisy.shape, lambda i, s, f: (0, 0, 0, 0)),
            pl.BlockSpec((1, chunks, halves, 128), lambda i, s, f: (lax.rem(s[0], CSLOTS), 0, 0, 0)),
        ],
        out_specs=[
            pl.BlockSpec((rows, 2, cols, channels), lambda i, s, f: (0, 0, 0, 0)),
            pl.BlockSpec((halo, channels), lambda i, s, f: (0, 0)),
            pl.BlockSpec((halo, channels), lambda i, s, f: (0, 0)),
            pl.BlockSpec((tokens, 256), lambda i, s, f: (0, 0)),
        ],
        scratch_shapes=[
            pltpu.VMEM((tiles * rows, 128), F32),
            pltpu.VMEM(((frames + 1) * chunks * halves + 2 * tokens, 128), F32),
        ],
    )
    return pl.pallas_call(
        prepare_kernel,
        grid_spec=grid_spec,
        out_shape=[
            jax.ShapeDtypeStruct((rows, 2, cols, channels), BF),
            jax.ShapeDtypeStruct((halo, channels), BF),
            jax.ShapeDtypeStruct((halo, channels), BF),
            jax.ShapeDtypeStruct((tokens, 256), BF),
        ],
        compiler_params=params(1),
        cost_estimate=pl.CostEstimate(
            flops=rows * width, bytes_accessed=6 * rows * width, transcendentals=0
        ),
        name="prepare",
    )(span_index, cache_flags, tiled(feature_cache[:, 0]), noisy, tiled(latent_cache[:, 0]))


def shift_down(array):
    moved_rows = pltpu.roll(array, 1, axis=0)
    rows = lax.broadcasted_iota(jnp.int32, array.shape, 0)
    return jnp.where(rows == 0, 0.0, moved_rows)


def shift_up(array):
    count = array.shape[0]
    moved_rows = pltpu.roll(array, count - 1, axis=0)
    rows = lax.broadcasted_iota(jnp.int32, array.shape, 0)
    return jnp.where(rows == count - 1, 0.0, moved_rows)


def cached_kernel(own_ref, above_ref, below_ref, weight_ref, out_ref, var):
    rows, _, cols, channels = own_ref.shape
    for r in range(rows + 2):
        if r == 0:
            even, odd = above_ref[:cols], above_ref[cols : 2 * cols]
        elif r == rows + 1:
            even, odd = below_ref[:cols], below_ref[cols : 2 * cols]
        else:
            even, odd = own_ref[r - 1, 0], own_ref[r - 1, 1]
        var[0, r] = shift_down(odd.astype(F32)).astype(BF)
        var[1, r] = even
        var[2, r] = odd
        var[3, r] = shift_up(even.astype(F32)).astype(BF)

    def contribute(f, base):
        for r in range(0, rows, 2):
            sides = []
            for b in range(2):
                total = None
                for h in range(3):
                    left = jnp.concatenate(
                        [
                            var[b + w, r + h : r + h + 2].reshape(2 * cols, channels)
                            for w in range(3)
                        ],
                        axis=1,
                    )
                    start = pl.multiple_of(base + h * 3 * channels, 128)
                    part = dot_last(left, weight_ref[:, pl.ds(start, 3 * channels)])
                    total = part if total is None else total + part
                sides.append(total)
            both = jnp.concatenate(sides, axis=1).astype(BF)
            out_ref[f, r : r + 2] = both.reshape(2, cols, both.shape[1])

    head = lax.axis_index("head")
    contribute(0, head * (9 * channels))

    @pl.when(head == 0)
    def _():
        out_ref[1] = jnp.zeros(out_ref.shape[1:], BF)

    @pl.when(head != 0)
    def _():
        contribute(1, 0)


def cached(own, above, below, weight):
    rows, _, cols, channels = own.shape
    return pl.pallas_call(
        cached_kernel,
        in_specs=[whole()] * 4,
        out_specs=whole(),
        out_shape=jax.ShapeDtypeStruct((2, rows, cols, 2 * weight.shape[0]), BF),
        scratch_shapes=[pltpu.VMEM((4, rows + 2, cols, channels), BF)],
        compiler_params=params(),
        cost_estimate=pl.CostEstimate(
            flops=2 * 2 * rows * 2 * cols * 9 * channels * weight.shape[0],
            bytes_accessed=2 * (own.size + weight.size),
            transcendentals=0,
        ),
        name="cached",
    )(own, above, below, weight)


def mix_kernel(weight_ref, out_ref):
    channels = weight_ref.shape[1] // 9

    def tap(h, w):
        start = (h * 3 + w) * channels
        return weight_ref[:, start : start + channels].astype(F32)

    lines = {}
    for w in range(3):
        top, middle, bottom = tap(0, w), tap(1, w), tap(2, w)
        lines[0, 0, w] = top
        lines[0, 1, w] = middle + bottom
        lines[1, 0, w] = top + middle
        lines[1, 1, w] = bottom
    for a in range(2):
        for u in range(2):
            left, centre, right = [lines[a, u, w] for w in range(3)]
            mixed = ((left, centre + right), (left + centre, right))
            for b in range(2):
                for v in range(2):
                    start = (u * 2 + v) * channels
                    out_ref[0, a * 2 + b, :, start : start + channels] = mixed[b][v].astype(BF)


def mix(weight):
    out, height = weight.shape
    third = height // 3
    shape = (3, 4, out, third // 9 * 4)
    return pl.pallas_call(
        mix_kernel,
        grid=(3,),
        in_specs=[pl.BlockSpec((out, third), lambda t: (0, t))],
        out_specs=pl.BlockSpec((1,) + shape[1:], lambda t: (t, 0, 0, 0)),
        out_shape=jax.ShapeDtypeStruct(shape, BF),
        compiler_params=params(1),
        cost_estimate=pl.CostEstimate(
            flops=4 * weight.size, bytes_accessed=6 * weight.size, transcendentals=0
        ),
        name="mix",
    )(weight)


def spread(source_ref, var):
    frames, coarse = source_ref.shape[:2]
    for f in range(frames):
        for r in range(coarse):
            plain = source_ref[f, r]
            wide = plain.astype(F32)
            var[0, f, r] = shift_down(wide).astype(BF)
            var[1, f, r] = plain
            var[2, f, r] = shift_up(wide).astype(BF)


def taps(var, frames, a, b):
    coarse = var.shape[2]
    lines = []
    for frame in frames:
        for r in range(coarse - 2):
            lines.append(
                jnp.concatenate(
                    [var[b + v, frame, r + a + u] for u in range(2) for v in range(2)], axis=1
                )
            )
    return jnp.concatenate(lines, axis=0)


def own_kernel(source_ref, old_ref, new_ref, out_ref, var):
    step = pl.program_id(0)
    a = step // 2
    b = step % 2

    @pl.when(step == 0)
    def _():
        spread(source_ref, var)

    both = dot_last(taps(var, (0, 1), a, b), new_ref[0, 0])
    more = dot_last(taps(var, (0,), a, b), old_ref[0, 0])
    height = more.shape[0]
    shape = out_ref.shape[2:]
    out_ref[0, 0] = both[:height].reshape(shape)
    out_ref[0, 1] = (both[height:] + more).reshape(shape)


def own_part(activated, mixed):
    frames, coarse, cols, channels = activated.shape
    _, parities, width, depth = mixed.shape
    block = (1, 1, width, depth)
    shape = (parities, frames, coarse - 2, cols, width)
    return pl.pallas_call(
        own_kernel,
        grid=(parities,),
        in_specs=[
            pl.BlockSpec(activated.shape, lambda i: (0, 0, 0, 0)),
            pl.BlockSpec(block, lambda i: (1, i, 0, 0)),
            pl.BlockSpec(block, lambda i: (2, i, 0, 0)),
        ],
        out_specs=pl.BlockSpec((1,) + shape[1:], lambda i: (i, 0, 0, 0, 0)),
        out_shape=jax.ShapeDtypeStruct(shape, F32),
        scratch_shapes=[pltpu.VMEM((3, frames, coarse, cols, channels), BF)],
        compiler_params=params(1),
        cost_estimate=pl.CostEstimate(
            flops=2 * 3 * 2 * cols * depth * width * parities,
            bytes_accessed=2 * (activated.size + 2 * parities * width * depth),
            transcendentals=0,
        ),
        name="own_part",
    )(activated, mixed, mixed)


def prior_kernel(source_ref, cached_ref, own_ref, old_ref, new_ref, out_ref, var, total_ref, scr):
    parities, frames, coarse_rows, cols, width = total_ref.shape
    head = lax.axis_index("head")
    step = pl.program_id(0)
    a = step // 2
    b = step % 2

    @pl.when(head == 0)
    def _():
        total_ref[step] = own_ref[0]

    @pl.when(head != 0)
    def _():
        @pl.when(step == 0)
        def _():
            spread(source_ref, var)

        both = dot_last(taps(var, (0, 1), a, b), old_ref[0, 0])
        more = dot_last(taps(var, (1,), a, b), new_ref[0, 0])
        height = more.shape[0]
        shape = total_ref.shape[2:]
        total_ref[step, 0] = own_ref[0, 0] + (both[:height] + more).reshape(shape)
        total_ref[step, 1] = own_ref[0, 1] + both[height:].reshape(shape)

    @pl.when(step == parities - 1)
    def _():
        fine = 2 * coarse_rows
        pieces = 2 * width // 128
        keep = jnp.where(head == 0, 1.0, 0.0)
        for f in range(frames):
            for row in range(fine):
                side = (row % 2) * 2
                sides = [total_ref[side + n, f, row // 2] for n in range(2)]
                line = jnp.concatenate(sides, axis=1)
                extra = cached_ref[f, row].astype(F32) + source_ref[f, row].astype(F32)
                line = line + keep * extra
                for q in range(pieces):
                    scr[pl.ds(q * fine + row, cols, stride=pieces * fine), :] = line[
                        :, q * 128 : (q + 1) * 128
                    ]

            def pack(i, carry):
                for n in range(16):
                    at = i * 16 + n
                    tile = scr[pl.ds(pl.multiple_of(at * fine, fine), fine), :]
                    out_ref[f, at] = tile.astype(BF)
                return carry

            lax.fori_loop(0, out_ref.shape[1] // 16, pack, 0)


def prior_part(received, cached_sum, own_sum, mixed):
    frames, coarse, cols, channels = received.shape
    _, parities, width, depth = mixed.shape
    fine = 2 * (coarse - 2)
    tiles = cols * 2 * width // 128
    block = (1, 1, width, depth)
    out = pl.pallas_call(
        prior_kernel,
        grid=(parities,),
        in_specs=[
            pl.BlockSpec(received.shape, lambda i: (0, 0, 0, 0)),
            pl.BlockSpec(cached_sum.shape, lambda i: (0, 0, 0, 0)),
            pl.BlockSpec((1,) + own_sum.shape[1:], lambda i: (i, 0, 0, 0, 0)),
            pl.BlockSpec(block, lambda i: (0, i, 0, 0)),
            pl.BlockSpec(block, lambda i: (1, i, 0, 0)),
        ],
        out_specs=pl.BlockSpec((frames, tiles, fine, 128), lambda i: (0, 0, 0, 0)),
        out_shape=jax.ShapeDtypeStruct((frames, tiles, fine, 128), BF),
        scratch_shapes=[
            pltpu.VMEM((3, frames, coarse, cols, channels), BF),
            pltpu.VMEM(own_sum.shape, F32),
            pltpu.VMEM((tiles * fine, 128), F32),
        ],
        compiler_params=params(1),
        cost_estimate=pl.CostEstimate(
            flops=2 * 3 * 2 * cols * depth * width * parities,
            bytes_accessed=2 * (received.size + 2 * parities * width * depth),
            transcendentals=0,
        ),
        name="prior_part",
    )(received, cached_sum, own_sum, mixed, mixed)
    return out.transpose(0, 2, 1, 3).reshape(frames, fine, tiles * 128)


def latent_kernel(step_ref, parts_ref, own_ref, above_ref, below_ref, clean_ref, send_ref, out_ref, scr):
    sources, three, unit, lanes = parts_ref.shape
    cols = own_ref.shape[0]
    frames, chunks, halves = out_ref.shape[:3]
    groups = frames * halves
    group = lanes // groups
    features = sources * 128
    fraction = 1.0 - step_ref[0].astype(F32) / NSTEPS
    fraction = jnp.full((1, lanes), fraction, F32)
    level = SHIFT_FACTOR * fraction / (1.0 + (SHIFT_FACTOR - 1.0) * fraction)
    total = parts_ref[0].astype(F32)
    for source in range(1, sources):
        total = total + parts_ref[source].astype(F32)
    half = lax.broadcasted_iota(jnp.int32, (cols, lanes), 1) < lanes // 2
    first_group = lax.axis_index("head") == 0
    for k, small_ref in ((0, above_ref), (1, own_ref), (2, below_ref)):
        small = small_ref[...] if k == 1 else small_ref[small_ref.shape[0] - cols :]
        sums = jnp.transpose(total[k, cols:unit])[:cols]
        scale = lax.rsqrt(sums / features + NORM_EPSILON)
        scale = jnp.where(half, scale[:, 0:1], scale[:, 1:2])
        velocity = total[k, :cols] * scale
        clean = (small[:, :lanes].astype(F32) - level * velocity).astype(BF)
        clean_ref[k] = clean
        if k == 1:
            scr[:cols, :] = clean.astype(F32)

        @pl.when(first_group)
        def _():
            send_ref[k] = clean

        @pl.when(jnp.logical_not(first_group))
        def _():
            send_ref[k] = small[:, lanes : 2 * lanes]

    parts = [scr[pl.ds(m, chunks, stride=groups), :] for m in range(groups)]
    for g in range(groups):
        total_line = None
        for m, part in enumerate(parts):
            term = jnp.where(lane_groups(part, group) == m, moved(part, group * (m - g)), 0.0)
            total_line = term if total_line is None else total_line + term
        f, a = g // halves, g % halves
        scr[pl.ds(cols + f * chunks * halves + a, chunks, stride=halves), :] = total_line
    for f in range(frames):
        for i in range(chunks):
            at = cols + (f * chunks + i) * halves
            out_ref[f, i] = scr[at : at + halves, :].astype(BF)


def latent(step_index, parts, own, above, below, frames, halves, chunks):
    sources, three, unit, lanes = parts.shape
    cols = own.shape[0]
    shape = jax.ShapeDtypeStruct((three, cols, lanes), BF)
    return pl.pallas_call(
        latent_kernel,
        in_specs=[smem(), whole(), whole(), whole(), whole()],
        out_specs=[whole(), whole(), whole()],
        out_shape=[shape, shape, jax.ShapeDtypeStruct((frames, chunks, halves, 128), BF)],
        scratch_shapes=[pltpu.VMEM((cols + frames * chunks * halves, lanes), F32)],
        compiler_params=params(0, 8),
        cost_estimate=pl.CostEstimate(
            flops=2 * parts.size, bytes_accessed=2 * parts.size, transcendentals=0
        ),
        name="latent",
    )(step_index, parts, own, above, below)


def first_kernel(
    clean_ref, received_ref, own_ref, above_ref, below_ref, weight_ref, gain_ref, cached_ref, act_ref, send_ref, left, padded, scr
):
    three, cols, lanes = clean_ref.shape
    frames, coarse = act_ref.shape[:2]
    channels = act_ref.shape[3]
    group = lanes // 4
    slot = lanes // 2
    part = group // 2
    head = lax.axis_index("head")
    three_taps = weight_ref.shape[0] // 9
    gap = jnp.zeros((slot - three_taps, channels), BF)
    for n in range(9):
        padded[n * slot : n * slot + three_taps, :] = weight_ref[
            n * three_taps : (n + 1) * three_taps, :
        ]
        padded[n * slot + three_taps : (n + 1) * slot, :] = gap
    padded[9 * slot :, :] = jnp.zeros((slot, channels), BF)
    gains = gain_ref[...].astype(F32)
    gain = jnp.concatenate([gains[q : q + 1] for q in range(gains.shape[0])], axis=1)
    cached_old = jnp.concatenate(
        [
            above_ref[above_ref.shape[0] - cols :, lanes : 2 * lanes].astype(F32),
            own_ref[:, lanes : 2 * lanes].astype(F32),
            below_ref[below_ref.shape[0] - cols :, lanes : 2 * lanes].astype(F32),
        ],
        axis=0,
    )
    clean = jnp.concatenate([clean_ref[k].astype(F32) for k in range(three)], axis=0)
    arrived = jnp.concatenate([received_ref[k].astype(F32) for k in range(three)], axis=0)
    lane = lax.broadcasted_iota(jnp.int32, clean.shape, 1)
    line = lax.broadcasted_iota(jnp.int32, clean.shape, 0)
    at = lax.rem(line, cols)
    older = jnp.where(
        head == 0, jnp.where(lane < lanes // 2, cached_old, arrived), arrived
    )
    pieces = {}
    for source, x in enumerate((older, clean)):
        height = x.shape[0]
        before = jnp.where(at == 0, 0.0, pltpu.roll(x, 1, axis=0))
        after = jnp.where(at == cols - 1, 0.0, pltpu.roll(x, height - 1, axis=0))
        for f in range(2):
            for a in range(2):
                off = f * (lanes // 2) + a * group
                for side in range(2):
                    base = side * slot

                    low = lane - base
                    even = jnp.where(
                        (low >= 0) & (low < part),
                        moved(before, base - off - part),
                        jnp.where(
                            (low >= part) & (low < 3 * part), moved(x, base + part - off), 0.0
                        ),
                    )
                    odd = jnp.where(
                        (low >= 0) & (low < 2 * part),
                        moved(x, base - off),
                        jnp.where(
                            (low >= 2 * part) & (low < 3 * part),
                            moved(after, base + 2 * part - off),
                            0.0,
                        ),
                    )
                    pieces[source * 2 + f, a, side, 0] = even
                    pieces[source * 2 + f, a, side, 1] = odd

    def piece(p, fo, ro, n):
        frame = fo + n // 3
        row = ro + n % 3
        k = row // 2
        return pieces[frame, row % 2, n % 2, p][k * cols : (k + 1) * cols]

    for p in range(2):
        for fo in range(frames):
            for ro in range(coarse):
                start = ((p * frames + fo) * coarse + ro) * cols
                for j in range(5):
                    block = piece(p, fo, ro, 2 * j)
                    if 2 * j + 1 < 9:
                        block = block + piece(p, fo, ro, 2 * j + 1)
                    left[start : start + cols, j * lanes : (j + 1) * lanes] = block.astype(BF)

    feat = dot(left[...], padded[...])
    mean_square = jnp.mean(feat * feat, axis=-1, keepdims=True)
    normed = feat * lax.rsqrt(mean_square + NORM_EPSILON) * gain
    active = normed / (1.0 + jnp.exp(-normed))
    slab = lax.axis_index("seq")
    last = lax.axis_size("seq") - 1
    keep_first = jnp.where(slab == 0, 0.0, 1.0)
    keep_last = jnp.where(slab == last, 0.0, 1.0)
    for p in range(2):
        for fo in range(frames):
            for ro in range(coarse):
                start = ((p * frames + fo) * coarse + ro) * cols
                block = active[start : start + cols]
                if ro == 0:
                    block = block * keep_first
                if ro == coarse - 1:
                    block = block * keep_last
                to = (fo * coarse + ro) * 2 * cols + p
                for q in range(channels // 128):
                    scr[q, pl.ds(to, cols, stride=2), :] = block[:, q * 128 : (q + 1) * 128]
    for fo in range(frames):
        for ro in range(coarse):
            to = (fo * coarse + ro) * 2 * cols
            for q in range(channels // 128):
                act_ref[fo, ro, :, q * 128 : (q + 1) * 128] = scr[q, to : to + 2 * cols, :].astype(BF)

    @pl.when(head == 0)
    def _():
        send_ref[...] = act_ref[...]

    @pl.when(head != 0)
    def _():
        send_ref[...] = cached_ref[...]


def first(clean, received, own, above, below, weight, gain, cached_sum):
    three, cols, lanes = clean.shape
    shape = jax.ShapeDtypeStruct(cached_sum.shape, BF)
    frames, coarse, wide, channels = cached_sum.shape
    height = frames * coarse * wide
    return pl.pallas_call(
        first_kernel,
        in_specs=[whole()] * 8,
        out_specs=[whole(), whole()],
        out_shape=[shape, shape],
        scratch_shapes=[
            pltpu.VMEM((height, 5 * lanes), BF),
            pltpu.VMEM((5 * lanes, channels), BF),
            pltpu.VMEM((channels // 128, height, 128), F32),
        ],
        compiler_params=params(),
        cost_estimate=pl.CostEstimate(
            flops=2 * height * weight.size, bytes_accessed=4 * cached_sum.size, transcendentals=height * channels
        ),
        name="first",
    )(clean, received, own, above, below, weight, gain, cached_sum)


def swapped(array, axis):
    return lax.ppermute(array, axis, [(0, 1), (1, 0)])


def body(
    queries,
    keys,
    values,
    final_gain,
    out_weight,
    noisy_latent,
    step_index,
    span_index,
    cache_flags,
    latent_cache,
    feature_cache,
    first_weight,
    first_gain,
    second_weight,
):
    channels = first_weight.shape[1]
    slabs = lax.axis_size("seq")
    frames, halves, width = noisy_latent.shape
    second = second_weight.T

    own_frame, up, down, small = prepare(
        span_index, cache_flags, feature_cache, noisy_latent, latent_cache, channels
    )
    above = lax.ppermute(down, "seq", [(i, i + 1) for i in range(slabs - 1)])
    below = lax.ppermute(up, "seq", [(i + 1, i) for i in range(slabs - 1)])

    sent = attention(queries, keys, values, final_gain, out_weight)
    parts = lax.all_to_all(sent, "seq", 0, 0, tiled=True)
    mixed = mix(second)
    cached_sum = cached(own_frame, above, below, second)

    clean, send, out = latent(step_index, parts, small, above, below, frames, halves, width // 128)
    received = swapped(send, "head")
    activated, send = first(
        clean, received, small, above, below, first_weight, first_gain.reshape(-1, 128), cached_sum
    )
    arrived = swapped(send, "head")
    own_sum = own_part(activated, mixed)
    decoded = prior_part(arrived, cached_sum, own_sum, mixed)
    return (out.transpose(0, 2, 1, 3).reshape(frames, halves, width), decoded)


def solution(mesh):
    in_specs = (
        P(("grp", "head"), None, None, "seq"),
        P("grp", None, None, "seq"),
        P("grp", None, None, "seq"),
        P(),
        P(),
        P(("grp", "head"), "seq", None),
        P("grp"),
        P("grp"),
        P("grp", None, None),
        P("grp", "head", "seq", None),
        P("grp", "head", "seq", None),
        P(),
        P(),
        P(),
    )
    out_specs = (P(("grp", "head"), "seq", None), P(("grp", "head"), "seq", None))
    return jax.shard_map(body, mesh=mesh, in_specs=in_specs, out_specs=out_specs, check_vma=False)
```

```python
import jax
import jax.numpy as jnp
from jax import lax
from jax.experimental import pallas as pl
from jax.experimental.pallas import tpu as pltpu
from jax.sharding import PartitionSpec as P

NSTEPS = 16
CSLOTS = 2
SHIFT_FACTOR = 5.0
NORM_EPSILON = 1e-06
BF = jnp.bfloat16
F32 = jnp.float32
LAST = (((1,), (1,)), ((), ()))


def params(dims=0, mib=12):
    semantics = ("arbitrary",) * dims if dims else None
    return pltpu.CompilerParams(dimension_semantics=semantics, vmem_limit_bytes=mib << 20)


def dot(left, right):
    return jnp.dot(left, right, preferred_element_type=F32)


def dot_last(left, right):
    return lax.dot_general(left, right, LAST, preferred_element_type=F32)


def far(array):
    return pltpu.with_memory_space_constraint(array, pltpu.HBM)


def far_spec():
    return pl.BlockSpec(memory_space=pltpu.HBM)


def whole():
    return pl.BlockSpec(memory_space=pltpu.VMEM)


def attention_kernel(
    code_ref,
    flags_hbm,
    q_hbm,
    k_hbm,
    v_hbm,
    gain_hbm,
    weight_hbm,
    cache_hbm,
    noisy_hbm,
    latent_hbm,
    out_ref,
    facts_ref,
    cache_ref,
    noisy_ref,
    latent_ref,
    flags_ref,
    q_ref,
    k_ref,
    v_ref,
    gain_ref,
    weight_ref,
    sems,
    *,
    cols,
    rows,
):
    slab = lax.axis_index("seq")
    head = lax.axis_index("head")
    frames, query_count, head_size = q_ref.shape
    rows_total = query_count // cols
    count = [0]

    def load(source, target):
        copy = pltpu.make_async_copy(source, target, sems.at[count[0]])
        count[0] += 1
        copy.start()
        return copy

    slot = lax.rem(code_ref[0] // NSTEPS, CSLOTS)
    key_copies = [load(q_hbm, q_ref), load(k_hbm, k_ref)]
    value_copies = [load(v_hbm, v_ref), load(gain_hbm, gain_ref), load(weight_hbm, weight_ref)]
    later = [
        load(flags_hbm, flags_ref),
        load(cache_hbm.at[slot], cache_ref),
        load(latent_hbm.at[slot], latent_ref),
        load(noisy_hbm, noisy_ref),
    ]
    edge = jnp.zeros(out_ref.shape[2:], BF)
    out_ref[0, 0] = edge
    out_ref[rows_total - 1, 2] = edge
    for copy in key_copies + value_copies:
        copy.wait()

    scale = 1.4426950408889634 / head_size**0.5
    keys = k_ref[...]
    values = jnp.concatenate([v_ref[...], jnp.ones_like(v_ref[...])], axis=1)
    gains = gain_ref[...].astype(F32)
    chosen = lax.broadcasted_iota(jnp.int32, gains.shape, 0) == slab
    gain = jnp.sum(jnp.where(chosen, gains, 0.0), axis=0, keepdims=True)
    start = pl.multiple_of(slab * head_size, head_size)
    weight = weight_ref[:, pl.ds(start, head_size)]
    none = jnp.zeros_like(weight)
    line_of = lax.broadcasted_iota(jnp.int32, (8, head_size), 0)

    def block(step):
        total = None
        squares = []
        for f in range(frames):
            at = step * (rows * cols)
            if not isinstance(step, int):
                at = pl.multiple_of(at, 16)
            scores = dot_last(q_ref[f, pl.ds(at, rows * cols), :], keys)
            row_max = jnp.max(scores, axis=1, keepdims=True)
            weights = jnp.exp2((scores - row_max) * scale).astype(BF)
            blended = dot(weights, values)
            attended = (blended[:, :head_size] / blended[:, head_size:]).astype(BF).astype(F32)
            side = [none] * frames
            side[f] = weight
            part = dot_last((attended * gain).astype(BF), jnp.concatenate(side, axis=0))
            total = part if total is None else total + part
            squares.append(attended * attended)
        for r in range(rows):
            sums = None
            for f in range(frames):
                piece = squares[f][r * cols : (r + 1) * cols].astype(BF)
                line = dot_last((line_of == f).astype(F32).astype(BF), piece)
                sums = line if sums is None else sums + line
            lanes = total.shape[1]
            sums = jnp.concatenate([sums, jnp.zeros((8, lanes - cols), F32)], axis=1)
            unit = jnp.concatenate([total[r * cols : (r + 1) * cols], sums], axis=0).astype(BF)
            row = step * rows + r
            out_ref[row, 1] = unit
            if isinstance(step, int):
                if row + 1 < rows_total:
                    out_ref[row + 1, 0] = unit
                if row > 0:
                    out_ref[row - 1, 2] = unit
            else:

                @pl.when(row + 1 < rows_total)
                def _():
                    out_ref[jnp.minimum(row + 1, rows_total - 1), 0] = unit

                @pl.when(row > 0)
                def _():
                    out_ref[jnp.maximum(row - 1, 0), 2] = unit

    steps = rows_total // rows
    if steps <= 2:
        for step in range(steps):
            block(step)
    else:

        def one(step, carry):
            block(step)
            return carry

        lax.fori_loop(0, steps, one, 0)

    for copy in later:
        copy.wait()
    fraction = 1.0 - lax.rem(code_ref[0], NSTEPS).astype(F32) / NSTEPS
    fraction = jnp.full((1, 128), fraction, F32)
    facts_ref[0:1, :] = SHIFT_FACTOR * fraction / (1.0 + (SHIFT_FACTOR - 1.0) * fraction)
    coarse = noisy_ref.shape[2]
    for r in range(coarse):
        flag = flags_ref[slot, head, slab * coarse + r].astype(F32)
        facts_ref[1 + r : 2 + r, :] = jnp.full((1, 128), flag, F32)


def attention(
    queries,
    keys,
    values,
    final_gain,
    out_weight,
    code,
    cache_flags,
    feature_cache,
    noisy_latent,
    latent_cache,
):
    frames, rows_total, cols, head_size = queries.shape
    q = queries.reshape(frames, rows_total * cols, head_size)
    k = keys.reshape(-1, head_size)
    v = values.reshape(-1, head_size)
    gains = final_gain.reshape(-1, head_size)
    weight = out_weight.T
    rows = 4 if rows_total % 4 == 0 else rows_total
    lanes = frames * weight.shape[0]
    unit = cols + 8
    cache = tiled(feature_cache[:, 0])
    noisy = tiled(noisy_latent)
    latents = tiled(latent_cache[:, 0])

    def kernel(*refs):
        attention_kernel(*refs, cols=cols, rows=rows)

    count = frames * rows_total * cols
    shapes = [
        ((rows_total, 3, unit, lanes), BF),
        ((8, 128), F32),
        (cache.shape[1:], BF),
        (noisy.shape, BF),
        (latents.shape[1:], BF),
    ]
    return pl.pallas_call(
        kernel,
        in_specs=[pl.BlockSpec(memory_space=pltpu.SMEM)]
        + [far_spec()] * 9,
        out_specs=[whole()] * len(shapes),
        out_shape=[pltpu.VMEM(shape, kind) for shape, kind in shapes],
        scratch_shapes=[
            pltpu.SMEM(cache_flags.shape, jnp.int32),
            pltpu.VMEM(q.shape, BF),
            pltpu.VMEM(k.shape, BF),
            pltpu.VMEM(v.shape, BF),
            pltpu.VMEM(gains.shape, BF),
            pltpu.VMEM(weight.shape, BF),
            pltpu.SemaphoreType.DMA((9,)),
        ],
        compiler_params=params(0, 16),
        cost_estimate=pl.CostEstimate(
            flops=6 * count * k.shape[0] * head_size,
            bytes_accessed=2 * (q.size + k.size + v.size),
            transcendentals=count * k.shape[0],
        ),
        name="attention",
    )(
        code,
        *[
            far(array)
            for array in (
                cache_flags,
                q,
                k,
                v,
                gains,
                weight,
                cache,
                noisy,
                latents,
            )
        ]
    )


def lane_groups(array, group):
    return lax.broadcasted_iota(jnp.int32, array.shape, 1) // group


def moved(array, shift):
    lanes = array.shape[1]
    shift = shift % lanes
    return pltpu.roll(array, shift, axis=1) if shift else array


def prepare_kernel(facts_ref, cache_ref, noisy_ref, latent_ref, own_ref, up_ref, down_ref, small_ref, scr, lat):
    tiles, rows, lanes = cache_ref.shape
    cols, channels = own_ref.shape[2:]
    pieces = channels // lanes
    coarse = rows // 2
    flags = [facts_ref[1 + r : 2 + r, :] for r in range(coarse)]
    whole_column = 2 * pieces * rows

    frames, chunks, halves = noisy_ref.shape[:3]
    groups = frames * halves
    group = lanes // groups
    for f in range(frames + 1):
        for i in range(chunks):
            tile = latent_ref[i] if f == frames else noisy_ref[f, i]
            lat[pl.ds((f * chunks + i) * halves, halves), :] = tile.astype(F32)
    lines = [
        [lat[pl.ds(f * chunks * halves + a, chunks, stride=halves), :] for a in range(halves)]
        for f in range(frames + 1)
    ]
    noisy = [lines[f][a] for f in range(frames) for a in range(halves)]
    old = [lines[frames][a] * flags[a] for f in range(frames) for a in range(halves)]
    base = (frames + 1) * chunks * halves
    tokens = chunks * groups
    for n, parts in enumerate((noisy, old)):
        at = base + n * tokens
        for m in range(groups):
            total = None
            for g, part in enumerate(parts):
                term = jnp.where(lane_groups(part, group) == g, moved(part, group * (g - m)), 0.0)
                total = term if total is None else total + term
            lat[pl.ds(at + m, chunks, stride=groups), :] = total
        block = lat[at : at + tokens, :].astype(BF)
        small_ref[:, n * lanes : (n + 1) * lanes] = block
        up_ref[2 * cols :, n * lanes : (n + 1) * lanes] = block
        down_ref[2 * cols :, n * lanes : (n + 1) * lanes] = block
    rest = jnp.zeros((tokens, channels - 2 * lanes), BF)
    up_ref[2 * cols :, 2 * lanes :] = rest
    down_ref[2 * cols :, 2 * lanes :] = rest

    pad = jnp.zeros((whole_column, lanes), F32)
    scr[:whole_column, :] = pad
    scr[whole_column + tiles * rows :, :] = pad

    def unpack(i, carry):
        for n in range(16):
            at = i * 16 + n
            to = pl.multiple_of(whole_column + at * rows, rows)
            scr[pl.ds(to, rows), :] = cache_ref[at].astype(F32)
        return carry

    lax.fori_loop(0, tiles // 16, unpack, 0)
    for r in range(rows):
        for n in range(4):
            for q in range(pieces):
                column = whole_column * ((n + 1) // 2) + ((n + 1) % 2) * pieces * rows
                start = column + q * rows + r
                piece = scr[pl.ds(start, cols, stride=whole_column), :]
                piece = (piece * flags[r // 2]).astype(BF)
                own_ref[n, r, :, q * lanes : (q + 1) * lanes] = piece
                if n in (1, 2):
                    to = slice((n - 1) * cols, n * cols)
                    if r == 0:
                        up_ref[to, q * lanes : (q + 1) * lanes] = piece
                    if r == rows - 1:
                        down_ref[to, q * lanes : (q + 1) * lanes] = piece


def tiled(array):
    *lead, rows, width = array.shape
    count = len(lead)
    view = array.reshape(*lead, rows, width // 128, 128)
    return view.transpose(*range(count), count + 1, count, count + 2)


def prepare(facts, cache, noisy, latents, channels):
    tiles, rows, lanes = cache.shape
    cols = tiles * lanes // channels // 2
    frames, chunks, halves = noisy.shape[:3]
    tokens = chunks * frames * halves
    halo = 2 * cols + tokens
    return pl.pallas_call(
        prepare_kernel,
        in_specs=[whole()] * 4,
        out_specs=[whole()] * 4,
        out_shape=[
            jax.ShapeDtypeStruct((4, rows, cols, channels), BF),
            jax.ShapeDtypeStruct((halo, channels), BF),
            jax.ShapeDtypeStruct((halo, channels), BF),
            jax.ShapeDtypeStruct((tokens, 256), BF),
        ],
        scratch_shapes=[
            pltpu.VMEM((tiles * rows + 4 * channels // lanes * rows, lanes), F32),
            pltpu.VMEM(((frames + 1) * chunks * halves + 2 * tokens, lanes), F32),
        ],
        compiler_params=params(),
        cost_estimate=pl.CostEstimate(
            flops=cache.size, bytes_accessed=6 * cache.size, transcendentals=0
        ),
        name="prepare",
    )(facts, cache, noisy, latents)


def shift_down(array):
    moved_rows = pltpu.roll(array, 1, axis=0)
    rows = lax.broadcasted_iota(jnp.int32, array.shape, 0)
    return jnp.where(rows == 0, 0.0, moved_rows)


def shift_up(array):
    count = array.shape[0]
    moved_rows = pltpu.roll(array, count - 1, axis=0)
    rows = lax.broadcasted_iota(jnp.int32, array.shape, 0)
    return jnp.where(rows == count - 1, 0.0, moved_rows)


def cached_sum(line, rows, weight):
    lines = []
    for b in range(2):
        for r in rows:
            lines.append(
                jnp.concatenate(
                    [line(b + w, r + h - 1) for h in range(3) for w in range(3)], axis=1
                )
            )
    total = dot_last(jnp.concatenate(lines, axis=0), weight)
    half = total.shape[0] // 2
    return jnp.concatenate([total[:half], total[half:]], axis=1).astype(BF)


def slices(weight_hbm, weight_ref, sems, count):
    depth = weight_ref.shape[2]
    copies = []
    for t in range(count):
        source = weight_hbm.at[:, pl.ds(t * depth, depth)]
        copies.append(pltpu.make_async_copy(source, weight_ref.at[t], sems.at[t]))
    return copies


def mix_third(weight_ref, out_ref, t):
    channels = weight_ref.shape[2] // 9

    def tap(h, w):
        start = (h * 3 + w) * channels
        return weight_ref[t, :, start : start + channels].astype(F32)

    lines = {}
    for w in range(3):
        top, middle, bottom = tap(0, w), tap(1, w), tap(2, w)
        lines[0, 0, w] = top
        lines[0, 1, w] = middle + bottom
        lines[1, 0, w] = top + middle
        lines[1, 1, w] = bottom
    for a in range(2):
        for u in range(2):
            left, centre, right = [lines[a, u, w] for w in range(3)]
            mixed = ((left, centre + right), (left + centre, right))
            for b in range(2):
                for v in range(2):
                    start = (u * 2 + v) * channels
                    out_ref[t, a * 2 + b, :, start : start + channels] = mixed[b][v].astype(BF)


def mix_kernel(own_ref, weight_hbm, mixed_hbm, middle_ref, weight_ref, mixed_ref, sems, out_sems):
    rows = own_ref.shape[1]
    head = lax.axis_index("head")
    inner = range(1, rows - 1)
    copies = slices(weight_hbm, weight_ref, sems, 3)
    for copy in copies:
        copy.start()

    def line(n, r):
        return own_ref[n, r]

    outs = [pltpu.make_async_copy(mixed_ref.at[t], mixed_hbm.at[t], out_sems.at[t]) for t in range(3)]
    shape = middle_ref.shape[1:]
    for t in range(3):
        copies[t].wait()
        mix_third(weight_ref, mixed_ref, t)
        outs[t].start()
        if t == 0:

            @pl.when(head == 0)
            def _():
                middle_ref[0] = cached_sum(line, inner, weight_ref[0]).reshape(shape)
                middle_ref[1] = jnp.zeros(shape, BF)

            @pl.when(head != 0)
            def _():
                middle_ref[1] = cached_sum(line, inner, weight_ref[0]).reshape(shape)

        if t == 1:

            @pl.when(head != 0)
            def _():
                middle_ref[0] = cached_sum(line, inner, weight_ref[1]).reshape(shape)

    for copy in outs:
        copy.wait()


def mix(own, weight):
    _, rows, cols, channels = own.shape
    out, height = weight.shape
    third = height // 3
    shape = (3, 4, out, third // 9 * 4)
    return pl.pallas_call(
        mix_kernel,
        in_specs=[whole(), far_spec()],
        out_specs=[far_spec(), whole()],
        out_shape=[
            pltpu.HBM(shape, BF),
            jax.ShapeDtypeStruct((2, rows - 2, cols, 2 * out), BF),
        ],
        scratch_shapes=[
            pltpu.VMEM((3, out, third), BF),
            pltpu.VMEM(shape, BF),
            pltpu.SemaphoreType.DMA((3,)),
            pltpu.SemaphoreType.DMA((3,)),
        ],
        compiler_params=params(0, 24),
        cost_estimate=pl.CostEstimate(
            flops=2 * 2 * 2 * 2 * cols * third * out,
            bytes_accessed=6 * weight.size,
            transcendentals=0,
        ),
        name="mix",
    )(own, far(weight))


def edge_kernel(own_ref, above_ref, below_ref, weight_hbm, out_ref, var, weight_ref, sems):
    _, rows, cols, channels = own_ref.shape
    head = lax.axis_index("head")
    first_copy, second_copy = slices(weight_hbm, weight_ref, sems, 2)
    first_copy.start()

    @pl.when(head != 0)
    def _():
        second_copy.start()

    for n, rim in enumerate((above_ref, below_ref)):
        even, odd = rim[:cols], rim[cols : 2 * cols]
        var[n, 0] = shift_down(odd.astype(F32)).astype(BF)
        var[n, 1] = even
        var[n, 2] = odd
        var[n, 3] = shift_up(even.astype(F32)).astype(BF)

    def line(n, r):
        if r < 0:
            return var[0, n]
        return var[1, n] if r == rows else own_ref[n, r]

    outer = (0, rows - 1)
    shape = out_ref.shape[1:]
    first_copy.wait()

    @pl.when(head == 0)
    def _():
        out_ref[0] = cached_sum(line, outer, weight_ref[0]).reshape(shape)
        out_ref[1] = jnp.zeros(shape, BF)

    @pl.when(head != 0)
    def _():
        out_ref[1] = cached_sum(line, outer, weight_ref[0]).reshape(shape)
        second_copy.wait()
        out_ref[0] = cached_sum(line, outer, weight_ref[1]).reshape(shape)


def edges(own, above, below, weight):
    _, rows, cols, channels = own.shape
    out, height = weight.shape
    return pl.pallas_call(
        edge_kernel,
        in_specs=[whole(), whole(), whole(), far_spec()],
        out_specs=whole(),
        out_shape=jax.ShapeDtypeStruct((2, 2, cols, 2 * out), BF),
        scratch_shapes=[
            pltpu.VMEM((2, 4, cols, channels), BF),
            pltpu.VMEM((2, out, height // 3), BF),
            pltpu.SemaphoreType.DMA((2,)),
        ],
        compiler_params=params(),
        cost_estimate=pl.CostEstimate(
            flops=2 * 2 * 2 * 2 * cols * 9 * channels * out,
            bytes_accessed=2 * (own.size + weight.size),
            transcendentals=0,
        ),
        name="edge",
    )(own, above, below, far(weight))


def spread(source_ref, var):
    frames, coarse = source_ref.shape[:2]
    for f in range(frames):
        for r in range(coarse):
            plain = source_ref[f, r]
            wide = plain.astype(F32)
            var[0, f, r] = shift_down(wide).astype(BF)
            var[1, f, r] = plain
            var[2, f, r] = shift_up(wide).astype(BF)


def taps(var, frames, a, b):
    coarse = var.shape[2]
    lines = []
    for frame in frames:
        for r in range(coarse - 2):
            lines.append(
                jnp.concatenate(
                    [var[b + v, frame, r + a + u] for u in range(2) for v in range(2)], axis=1
                )
            )
    return jnp.concatenate(lines, axis=0)


def own_kernel(source_ref, old_ref, new_ref, out_ref, var):
    step = pl.program_id(0)
    a = step // 2
    b = step % 2

    @pl.when(step == 0)
    def _():
        spread(source_ref, var)

    both = dot_last(taps(var, (0, 1), a, b), new_ref[0, 0])
    more = dot_last(taps(var, (0,), a, b), old_ref[0, 0])
    height = more.shape[0]
    shape = out_ref.shape[2:]
    out_ref[0, 0] = both[:height].reshape(shape)
    out_ref[0, 1] = (both[height:] + more).reshape(shape)


def own_part(activated, mixed):
    frames, coarse, cols, channels = activated.shape
    _, parities, width, depth = mixed.shape
    block = (1, 1, width, depth)
    shape = (parities, frames, coarse - 2, cols, width)
    return pl.pallas_call(
        own_kernel,
        grid=(parities,),
        in_specs=[
            pl.BlockSpec(activated.shape, lambda i: (0, 0, 0, 0)),
            pl.BlockSpec(block, lambda i: (1, i, 0, 0)),
            pl.BlockSpec(block, lambda i: (2, i, 0, 0)),
        ],
        out_specs=pl.BlockSpec((1,) + shape[1:], lambda i: (i, 0, 0, 0, 0)),
        out_shape=jax.ShapeDtypeStruct(shape, F32),
        scratch_shapes=[pltpu.VMEM((3, frames, coarse, cols, channels), BF)],
        compiler_params=params(1),
        cost_estimate=pl.CostEstimate(
            flops=2 * 3 * 2 * cols * depth * width * parities,
            bytes_accessed=2 * (activated.size + 2 * parities * width * depth),
            transcendentals=0,
        ),
        name="own_part",
    )(activated, far(mixed), far(mixed))


def prior_kernel(source_ref, middle_ref, edge_ref, own_ref, old_ref, new_ref, out_ref, var, total_ref, scr):
    parities, frames, coarse_rows, cols, width = total_ref.shape
    head = lax.axis_index("head")
    step = pl.program_id(0)
    a = step // 2
    b = step % 2

    @pl.when(head == 0)
    def _():
        total_ref[step] = own_ref[0]

    @pl.when(head != 0)
    def _():
        @pl.when(step == 0)
        def _():
            spread(source_ref, var)

        both = dot_last(taps(var, (0, 1), a, b), old_ref[0, 0])
        more = dot_last(taps(var, (1,), a, b), new_ref[0, 0])
        height = more.shape[0]
        shape = total_ref.shape[2:]
        total_ref[step, 0] = own_ref[0, 0] + (both[:height] + more).reshape(shape)
        total_ref[step, 1] = own_ref[0, 1] + both[height:].reshape(shape)

    @pl.when(step == parities - 1)
    def _():
        fine = 2 * coarse_rows
        pieces = 2 * width // 128
        keep = jnp.where(head == 0, 1.0, 0.0)
        for f in range(frames):
            for row in range(fine):
                side = (row % 2) * 2
                sides = [total_ref[side + n, f, row // 2] for n in range(2)]
                line = jnp.concatenate(sides, axis=1)
                if row in (0, fine - 1):
                    mine = edge_ref[f, min(row, 1)]
                else:
                    mine = middle_ref[f, row - 1]
                extra = mine.astype(F32) + source_ref[f, row].astype(F32)
                line = line + keep * extra
                for q in range(pieces):
                    scr[pl.ds(q * fine + row, cols, stride=pieces * fine), :] = line[
                        :, q * 128 : (q + 1) * 128
                    ]

            def pack(i, carry):
                for n in range(16):
                    at = i * 16 + n
                    tile = scr[pl.ds(pl.multiple_of(at * fine, fine), fine), :]
                    out_ref[f, at] = tile.astype(BF)
                return carry

            lax.fori_loop(0, out_ref.shape[1] // 16, pack, 0)


def prior_part(received, middle, edge, own_sum, mixed):
    frames, coarse, cols, channels = received.shape
    _, parities, width, depth = mixed.shape
    fine = 2 * (coarse - 2)
    tiles = cols * 2 * width // 128
    block = (1, 1, width, depth)
    out = pl.pallas_call(
        prior_kernel,
        grid=(parities,),
        in_specs=[
            pl.BlockSpec(received.shape, lambda i: (0, 0, 0, 0)),
            pl.BlockSpec(middle.shape, lambda i: (0, 0, 0, 0)),
            pl.BlockSpec(edge.shape, lambda i: (0, 0, 0, 0)),
            pl.BlockSpec((1,) + own_sum.shape[1:], lambda i: (i, 0, 0, 0, 0)),
            pl.BlockSpec(block, lambda i: (0, i, 0, 0)),
            pl.BlockSpec(block, lambda i: (1, i, 0, 0)),
        ],
        out_specs=pl.BlockSpec((frames, tiles, fine, 128), lambda i: (0, 0, 0, 0)),
        out_shape=jax.ShapeDtypeStruct((frames, tiles, fine, 128), BF),
        scratch_shapes=[
            pltpu.VMEM((3, frames, coarse, cols, channels), BF),
            pltpu.VMEM(own_sum.shape, F32),
            pltpu.VMEM((tiles * fine, 128), F32),
        ],
        compiler_params=params(1),
        cost_estimate=pl.CostEstimate(
            flops=2 * 3 * 2 * cols * depth * width * parities,
            bytes_accessed=2 * (received.size + 2 * parities * width * depth),
            transcendentals=0,
        ),
        name="prior_part",
    )(received, middle, edge, own_sum, far(mixed), far(mixed))
    return out.transpose(0, 2, 1, 3).reshape(frames, fine, tiles * 128)


def latent_kernel(facts_ref, parts_ref, own_ref, above_ref, below_ref, clean_ref, send_ref, out_ref, scr):
    sources, three, unit, lanes = parts_ref.shape
    cols = own_ref.shape[0]
    frames, chunks, halves = out_ref.shape[:3]
    groups = frames * halves
    group = lanes // groups
    features = sources * 128
    level = facts_ref[0:1, :]
    total = parts_ref[0].astype(F32)
    for source in range(1, sources):
        total = total + parts_ref[source].astype(F32)
    half = lax.broadcasted_iota(jnp.int32, (cols, lanes), 1) < lanes // 2
    first_group = lax.axis_index("head") == 0
    for k, small_ref in ((0, above_ref), (1, own_ref), (2, below_ref)):
        small = small_ref[...] if k == 1 else small_ref[small_ref.shape[0] - cols :]
        sums = jnp.transpose(total[k, cols:unit])[:cols]
        scale = lax.rsqrt(sums / features + NORM_EPSILON)
        scale = jnp.where(half, scale[:, 0:1], scale[:, 1:2])
        velocity = total[k, :cols] * scale
        clean = (small[:, :lanes].astype(F32) - level * velocity).astype(BF)
        clean_ref[k] = clean
        if k == 1:
            scr[:cols, :] = clean.astype(F32)

        @pl.when(first_group)
        def _():
            send_ref[k] = clean

        @pl.when(jnp.logical_not(first_group))
        def _():
            send_ref[k] = small[:, lanes : 2 * lanes]

    parts = [scr[pl.ds(m, chunks, stride=groups), :] for m in range(groups)]
    for g in range(groups):
        total_line = None
        for m, part in enumerate(parts):
            term = jnp.where(lane_groups(part, group) == m, moved(part, group * (m - g)), 0.0)
            total_line = term if total_line is None else total_line + term
        f, a = g // halves, g % halves
        scr[pl.ds(cols + f * chunks * halves + a, chunks, stride=halves), :] = total_line
    for f in range(frames):
        for i in range(chunks):
            at = cols + (f * chunks + i) * halves
            out_ref[f, i] = scr[at : at + halves, :].astype(BF)


def latent(facts, parts, own, above, below, frames, halves, chunks):
    sources, three, unit, lanes = parts.shape
    cols = own.shape[0]
    shape = jax.ShapeDtypeStruct((three, cols, lanes), BF)
    return pl.pallas_call(
        latent_kernel,
        in_specs=[whole()] * 5,
        out_specs=[whole(), whole(), whole()],
        out_shape=[shape, shape, jax.ShapeDtypeStruct((frames, chunks, halves, 128), BF)],
        scratch_shapes=[pltpu.VMEM((cols + frames * chunks * halves, lanes), F32)],
        compiler_params=params(0, 8),
        cost_estimate=pl.CostEstimate(
            flops=2 * parts.size, bytes_accessed=2 * parts.size, transcendentals=0
        ),
        name="latent",
    )(facts, parts, own, above, below)


def first_kernel(
    clean_ref, received_ref, own_ref, above_ref, below_ref, weight_ref, gain_ref, middle_ref, edge_ref, act_ref, send_ref, left, padded, scr
):
    three, cols, lanes = clean_ref.shape
    frames, coarse = act_ref.shape[:2]
    channels = act_ref.shape[3]
    group = lanes // 4
    slot = lanes // 2
    part = group // 2
    head = lax.axis_index("head")
    three_taps = weight_ref.shape[0] // 9
    gap = jnp.zeros((slot - three_taps, channels), BF)
    for n in range(9):
        padded[n * slot : n * slot + three_taps, :] = weight_ref[
            n * three_taps : (n + 1) * three_taps, :
        ]
        padded[n * slot + three_taps : (n + 1) * slot, :] = gap
    padded[9 * slot :, :] = jnp.zeros((slot, channels), BF)
    gains = gain_ref[...].astype(F32)
    gain = jnp.concatenate([gains[q : q + 1] for q in range(gains.shape[0])], axis=1)
    cached_old = jnp.concatenate(
        [
            above_ref[above_ref.shape[0] - cols :, lanes : 2 * lanes].astype(F32),
            own_ref[:, lanes : 2 * lanes].astype(F32),
            below_ref[below_ref.shape[0] - cols :, lanes : 2 * lanes].astype(F32),
        ],
        axis=0,
    )
    clean = jnp.concatenate([clean_ref[k].astype(F32) for k in range(three)], axis=0)
    arrived = jnp.concatenate([received_ref[k].astype(F32) for k in range(three)], axis=0)
    lane = lax.broadcasted_iota(jnp.int32, clean.shape, 1)
    line = lax.broadcasted_iota(jnp.int32, clean.shape, 0)
    at = lax.rem(line, cols)
    older = jnp.where(
        head == 0, jnp.where(lane < lanes // 2, cached_old, arrived), arrived
    )
    pieces = {}
    for source, x in enumerate((older, clean)):
        height = x.shape[0]
        before = jnp.where(at == 0, 0.0, pltpu.roll(x, 1, axis=0))
        after = jnp.where(at == cols - 1, 0.0, pltpu.roll(x, height - 1, axis=0))
        for f in range(2):
            for a in range(2):
                off = f * (lanes // 2) + a * group
                for side in range(2):
                    base = side * slot

                    low = lane - base
                    even = jnp.where(
                        (low >= 0) & (low < part),
                        moved(before, base - off - part),
                        jnp.where(
                            (low >= part) & (low < 3 * part), moved(x, base + part - off), 0.0
                        ),
                    )
                    odd = jnp.where(
                        (low >= 0) & (low < 2 * part),
                        moved(x, base - off),
                        jnp.where(
                            (low >= 2 * part) & (low < 3 * part),
                            moved(after, base + 2 * part - off),
                            0.0,
                        ),
                    )
                    pieces[source * 2 + f, a, side, 0] = even
                    pieces[source * 2 + f, a, side, 1] = odd

    def piece(p, fo, ro, n):
        frame = fo + n // 3
        row = ro + n % 3
        k = row // 2
        return pieces[frame, row % 2, n % 2, p][k * cols : (k + 1) * cols]

    for p in range(2):
        for fo in range(frames):
            for ro in range(coarse):
                start = ((p * frames + fo) * coarse + ro) * cols
                for j in range(5):
                    block = piece(p, fo, ro, 2 * j)
                    if 2 * j + 1 < 9:
                        block = block + piece(p, fo, ro, 2 * j + 1)
                    left[start : start + cols, j * lanes : (j + 1) * lanes] = block.astype(BF)

    feat = dot(left[...], padded[...])
    mean_square = jnp.mean(feat * feat, axis=-1, keepdims=True)
    normed = feat * lax.rsqrt(mean_square + NORM_EPSILON) * gain
    active = normed / (1.0 + jnp.exp(-normed))
    slab = lax.axis_index("seq")
    last = lax.axis_size("seq") - 1
    keep_first = jnp.where(slab == 0, 0.0, 1.0)
    keep_last = jnp.where(slab == last, 0.0, 1.0)
    for p in range(2):
        for fo in range(frames):
            for ro in range(coarse):
                start = ((p * frames + fo) * coarse + ro) * cols
                block = active[start : start + cols]
                if ro == 0:
                    block = block * keep_first
                if ro == coarse - 1:
                    block = block * keep_last
                to = (fo * coarse + ro) * 2 * cols + p
                for q in range(channels // 128):
                    scr[q, pl.ds(to, cols, stride=2), :] = block[:, q * 128 : (q + 1) * 128]
    for fo in range(frames):
        for ro in range(coarse):
            to = (fo * coarse + ro) * 2 * cols
            for q in range(channels // 128):
                act_ref[fo, ro, :, q * 128 : (q + 1) * 128] = scr[q, to : to + 2 * cols, :].astype(BF)

    @pl.when(head == 0)
    def _():
        send_ref[...] = act_ref[...]

    @pl.when(head != 0)
    def _():
        for fo in range(frames):
            send_ref[fo, 0] = edge_ref[fo, 0]
            send_ref[fo, coarse - 1] = edge_ref[fo, 1]
            for ro in range(1, coarse - 1):
                send_ref[fo, ro] = middle_ref[fo, ro - 1]


def first(clean, received, own, above, below, weight, gain, middle, edge):
    three, cols, lanes = clean.shape
    frames, inner, wide, channels = middle.shape
    coarse = inner + 2
    shape = jax.ShapeDtypeStruct((frames, coarse, wide, channels), BF)
    height = frames * coarse * wide
    return pl.pallas_call(
        first_kernel,
        in_specs=[whole()] * 9,
        out_specs=[whole(), whole()],
        out_shape=[shape, shape],
        scratch_shapes=[
            pltpu.VMEM((height, 5 * lanes), BF),
            pltpu.VMEM((5 * lanes, channels), BF),
            pltpu.VMEM((channels // 128, height, 128), F32),
        ],
        compiler_params=params(),
        cost_estimate=pl.CostEstimate(
            flops=2 * height * weight.size, bytes_accessed=8 * middle.size, transcendentals=height * channels
        ),
        name="first",
    )(clean, received, own, above, below, weight, gain, middle, edge)


def swapped(array, axis):
    return lax.ppermute(array, axis, [(0, 1), (1, 0)])


def body(
    queries,
    keys,
    values,
    final_gain,
    out_weight,
    noisy_latent,
    step_index,
    span_index,
    cache_flags,
    latent_cache,
    feature_cache,
    first_weight,
    first_gain,
    second_weight,
):
    channels = first_weight.shape[1]
    slabs = lax.axis_size("seq")
    frames, halves, width = noisy_latent.shape
    second = second_weight.T

    sent, facts, cache, noisy, latents = attention(
        queries,
        keys,
        values,
        final_gain,
        out_weight,
        span_index * NSTEPS + step_index,
        cache_flags,
        feature_cache,
        noisy_latent,
        latent_cache,
    )
    parts = lax.all_to_all(sent, "seq", 0, 0, tiled=True)
    own_frame, up, down, small = prepare(facts, cache, noisy, latents, channels)
    above = lax.ppermute(down, "seq", [(i, i + 1) for i in range(slabs - 1)])
    below = lax.ppermute(up, "seq", [(i + 1, i) for i in range(slabs - 1)])
    mixed, middle = mix(own_frame, second)
    above, below, middle = lax.optimization_barrier((above, below, middle))

    clean, send, out = latent(facts, parts, small, above, below, frames, halves, width // 128)
    edge = edges(own_frame, above, below, second)
    received = swapped(send, "head")
    activated, send = first(
        clean, received, small, above, below, first_weight, first_gain.reshape(-1, 128), middle, edge
    )
    arrived = swapped(send, "head")
    own_sum = own_part(activated, mixed)
    decoded = prior_part(arrived, middle, edge, own_sum, mixed)
    return (out.transpose(0, 2, 1, 3).reshape(frames, halves, width), decoded)


def solution(mesh):
    in_specs = (
        P(("grp", "head"), None, None, "seq"),
        P("grp", None, None, "seq"),
        P("grp", None, None, "seq"),
        P(),
        P(),
        P(("grp", "head"), "seq", None),
        P("grp"),
        P("grp"),
        P("grp", None, None),
        P("grp", "head", "seq", None),
        P("grp", "head", "seq", None),
        P(),
        P(),
        P(),
    )
    out_specs = (P(("grp", "head"), "seq", None), P(("grp", "head"), "seq", None))
    return jax.shard_map(body, mesh=mesh, in_specs=in_specs, out_specs=out_specs, check_vma=False)
```

```python
import jax
import jax.numpy as jnp
from jax import lax
from jax.experimental import pallas as pl
from jax.experimental.pallas import tpu as pltpu
from jax.sharding import PartitionSpec as P

NSTEPS = 16
CSLOTS = 2
SHIFT_FACTOR = 5.0
NORM_EPSILON = 1e-06
BF = jnp.bfloat16
F32 = jnp.float32
LAST = (((1,), (1,)), ((), ()))


def params(dims=0, mib=12):
    semantics = ("arbitrary",) * dims if dims else None
    return pltpu.CompilerParams(dimension_semantics=semantics, vmem_limit_bytes=mib << 20)


def dot(left, right):
    return jnp.dot(left, right, preferred_element_type=F32)


def dot_last(left, right):
    return lax.dot_general(left, right, LAST, preferred_element_type=F32)


def smem():
    return pl.BlockSpec(memory_space=pltpu.SMEM)


def far(array):
    return pltpu.with_memory_space_constraint(array, pltpu.HBM)


def far_spec():
    return pl.BlockSpec(memory_space=pltpu.HBM)


def whole():
    return pl.BlockSpec(memory_space=pltpu.VMEM)


def attention_kernel(
    flags_hbm,
    q_hbm,
    k_hbm,
    v_hbm,
    gain_hbm,
    weight_hbm,
    cache_hbm,
    noisy_hbm,
    latent_hbm,
    out_ref,
    facts_ref,
    cache_ref,
    noisy_ref,
    latent_ref,
    flags_ref,
    q_ref,
    k_ref,
    v_ref,
    gain_ref,
    weight_ref,
    sems,
    *,
    cols,
    rows,
):
    slab = lax.axis_index("seq")
    head = lax.axis_index("head")
    frames, query_count, head_size = q_ref.shape
    rows_total = query_count // cols
    count = [0]

    def load(source, target):
        copy = pltpu.make_async_copy(source, target, sems.at[count[0]])
        count[0] += 1
        copy.start()
        return copy

    key_copies = [load(q_hbm, q_ref), load(k_hbm, k_ref)]
    value_copies = [load(v_hbm, v_ref), load(gain_hbm, gain_ref), load(weight_hbm, weight_ref)]
    later = [
        load(flags_hbm, flags_ref),
        load(cache_hbm, cache_ref),
        load(latent_hbm, latent_ref),
        load(noisy_hbm, noisy_ref),
    ]
    edge = jnp.zeros(out_ref.shape[2:], BF)
    out_ref[0, 0] = edge
    out_ref[rows_total - 1, 2] = edge
    for copy in key_copies + value_copies:
        copy.wait()

    scale = 1.4426950408889634 / head_size**0.5
    keys = k_ref[...]
    values = jnp.concatenate([v_ref[...], jnp.ones_like(v_ref[...])], axis=1)
    gains = gain_ref[...].astype(F32)
    chosen = lax.broadcasted_iota(jnp.int32, gains.shape, 0) == slab
    gain = jnp.sum(jnp.where(chosen, gains, 0.0), axis=0, keepdims=True)
    start = pl.multiple_of(slab * head_size, head_size)
    weight = weight_ref[:, pl.ds(start, head_size)]
    none = jnp.zeros_like(weight)
    line_of = lax.broadcasted_iota(jnp.int32, (8, head_size), 0)

    def block(step):
        total = None
        squares = []
        for f in range(frames):
            at = step * (rows * cols)
            if not isinstance(step, int):
                at = pl.multiple_of(at, 16)
            scores = dot_last(q_ref[f, pl.ds(at, rows * cols), :], keys)
            row_max = jnp.max(scores, axis=1, keepdims=True)
            weights = jnp.exp2((scores - row_max) * scale).astype(BF)
            blended = dot(weights, values)
            attended = (blended[:, :head_size] / blended[:, head_size:]).astype(BF).astype(F32)
            side = [none] * frames
            side[f] = weight
            part = dot_last((attended * gain).astype(BF), jnp.concatenate(side, axis=0))
            total = part if total is None else total + part
            squares.append(attended * attended)
        for r in range(rows):
            sums = None
            for f in range(frames):
                piece = squares[f][r * cols : (r + 1) * cols].astype(BF)
                line = dot_last((line_of == f).astype(F32).astype(BF), piece)
                sums = line if sums is None else sums + line
            lanes = total.shape[1]
            sums = jnp.concatenate([sums, jnp.zeros((8, lanes - cols), F32)], axis=1)
            unit = jnp.concatenate([total[r * cols : (r + 1) * cols], sums], axis=0).astype(BF)
            row = step * rows + r
            out_ref[row, 1] = unit
            if isinstance(step, int):
                if row + 1 < rows_total:
                    out_ref[row + 1, 0] = unit
                if row > 0:
                    out_ref[row - 1, 2] = unit
            else:

                @pl.when(row + 1 < rows_total)
                def _():
                    out_ref[jnp.minimum(row + 1, rows_total - 1), 0] = unit

                @pl.when(row > 0)
                def _():
                    out_ref[jnp.maximum(row - 1, 0), 2] = unit

    steps = rows_total // rows
    if steps <= 2:
        for step in range(steps):
            block(step)
    else:

        def one(step, carry):
            block(step)
            return carry

        lax.fori_loop(0, steps, one, 0)

    for copy in later:
        copy.wait()
    slots, _, coarse, _ = latent_ref.shape
    for slot in range(slots):
        for r in range(coarse):
            flag = flags_ref[slot, head, slab * coarse + r].astype(F32)
            at = slot * coarse + r
            facts_ref[at : at + 1, :] = jnp.full((1, 128), flag, F32)


def attention(
    queries,
    keys,
    values,
    final_gain,
    out_weight,
    cache_flags,
    feature_cache,
    noisy_latent,
    latent_cache,
):
    frames, rows_total, cols, head_size = queries.shape
    q = queries.reshape(frames, rows_total * cols, head_size)
    k = keys.reshape(-1, head_size)
    v = values.reshape(-1, head_size)
    gains = final_gain.reshape(-1, head_size)
    weight = out_weight.T
    rows = 4 if rows_total % 4 == 0 else rows_total
    lanes = frames * weight.shape[0]
    unit = cols + 8
    cache = tiled(feature_cache[:, 0])
    noisy = tiled(noisy_latent)
    latents = tiled(latent_cache[:, 0])

    def kernel(*refs):
        attention_kernel(*refs, cols=cols, rows=rows)

    count = frames * rows_total * cols
    shapes = [
        ((rows_total, 3, unit, lanes), BF),
        ((8, 128), F32),
        (cache.shape, BF),
        (noisy.shape, BF),
        (latents.shape, BF),
    ]
    return pl.pallas_call(
        kernel,
        in_specs=[far_spec()] * 9,
        out_specs=[whole()] * len(shapes),
        out_shape=[pltpu.VMEM(shape, kind) for shape, kind in shapes],
        scratch_shapes=[
            pltpu.SMEM(cache_flags.shape, jnp.int32),
            pltpu.VMEM(q.shape, BF),
            pltpu.VMEM(k.shape, BF),
            pltpu.VMEM(v.shape, BF),
            pltpu.VMEM(gains.shape, BF),
            pltpu.VMEM(weight.shape, BF),
            pltpu.SemaphoreType.DMA((9,)),
        ],
        compiler_params=params(0, 16),
        cost_estimate=pl.CostEstimate(
            flops=6 * count * k.shape[0] * head_size,
            bytes_accessed=2 * (q.size + k.size + v.size),
            transcendentals=count * k.shape[0],
        ),
        name="attention",
    )(
        *[
            far(array)
            for array in (
                cache_flags,
                q,
                k,
                v,
                gains,
                weight,
                cache,
                noisy,
                latents,
            )
        ]
    )


def lane_groups(array, group):
    return lax.broadcasted_iota(jnp.int32, array.shape, 1) // group


def moved(array, shift):
    lanes = array.shape[1]
    shift = shift % lanes
    return pltpu.roll(array, shift, axis=1) if shift else array


def prepare_kernel(span_ref, facts_ref, cache_ref, noisy_ref, latent_ref, own_ref, up_ref, down_ref, small_ref, scr, lat):
    _, tiles, rows, lanes = cache_ref.shape
    cols, channels = own_ref.shape[2:]
    pieces = channels // lanes
    coarse = rows // 2
    slot = lax.rem(span_ref[0], CSLOTS)
    flags = [facts_ref[pl.ds(slot * coarse + r, 1), :] for r in range(coarse)]
    whole_column = 2 * pieces * rows

    frames, chunks, halves = noisy_ref.shape[:3]
    groups = frames * halves
    group = lanes // groups
    for f in range(frames + 1):
        for i in range(chunks):
            tile = latent_ref[slot, i] if f == frames else noisy_ref[f, i]
            lat[pl.ds((f * chunks + i) * halves, halves), :] = tile.astype(F32)
    lines = [
        [lat[pl.ds(f * chunks * halves + a, chunks, stride=halves), :] for a in range(halves)]
        for f in range(frames + 1)
    ]
    noisy = [lines[f][a] for f in range(frames) for a in range(halves)]
    old = [lines[frames][a] * flags[a] for f in range(frames) for a in range(halves)]
    base = (frames + 1) * chunks * halves
    tokens = chunks * groups
    for n, parts in enumerate((noisy, old)):
        at = base + n * tokens
        for m in range(groups):
            total = None
            for g, part in enumerate(parts):
                term = jnp.where(lane_groups(part, group) == g, moved(part, group * (g - m)), 0.0)
                total = term if total is None else total + term
            lat[pl.ds(at + m, chunks, stride=groups), :] = total
        block = lat[at : at + tokens, :].astype(BF)
        small_ref[:, n * lanes : (n + 1) * lanes] = block
        up_ref[2 * cols :, n * lanes : (n + 1) * lanes] = block
        down_ref[2 * cols :, n * lanes : (n + 1) * lanes] = block
    rest = jnp.zeros((tokens, channels - 2 * lanes), BF)
    up_ref[2 * cols :, 2 * lanes :] = rest
    down_ref[2 * cols :, 2 * lanes :] = rest

    pad = jnp.zeros((whole_column, lanes), F32)
    scr[:whole_column, :] = pad
    scr[whole_column + tiles * rows :, :] = pad

    def unpack(i, carry):
        for n in range(16):
            at = i * 16 + n
            to = pl.multiple_of(whole_column + at * rows, rows)
            scr[pl.ds(to, rows), :] = cache_ref[slot, at].astype(F32)
        return carry

    lax.fori_loop(0, tiles // 16, unpack, 0)
    for r in range(rows):
        for n in range(4):
            for q in range(pieces):
                column = whole_column * ((n + 1) // 2) + ((n + 1) % 2) * pieces * rows
                start = column + q * rows + r
                piece = scr[pl.ds(start, cols, stride=whole_column), :]
                piece = (piece * flags[r // 2]).astype(BF)
                own_ref[n, r, :, q * lanes : (q + 1) * lanes] = piece
                if n in (1, 2):
                    to = slice((n - 1) * cols, n * cols)
                    if r == 0:
                        up_ref[to, q * lanes : (q + 1) * lanes] = piece
                    if r == rows - 1:
                        down_ref[to, q * lanes : (q + 1) * lanes] = piece


def tiled(array):
    *lead, rows, width = array.shape
    count = len(lead)
    view = array.reshape(*lead, rows, width // 128, 128)
    return view.transpose(*range(count), count + 1, count, count + 2)


def prepare(span_index, facts, cache, noisy, latents, channels):
    _, tiles, rows, lanes = cache.shape
    cols = tiles * lanes // channels // 2
    frames, chunks, halves = noisy.shape[:3]
    tokens = chunks * frames * halves
    halo = 2 * cols + tokens
    return pl.pallas_call(
        prepare_kernel,
        in_specs=[smem()] + [whole()] * 4,
        out_specs=[whole()] * 4,
        out_shape=[
            jax.ShapeDtypeStruct((4, rows, cols, channels), BF),
            jax.ShapeDtypeStruct((halo, channels), BF),
            jax.ShapeDtypeStruct((halo, channels), BF),
            jax.ShapeDtypeStruct((tokens, 256), BF),
        ],
        scratch_shapes=[
            pltpu.VMEM((tiles * rows + 4 * channels // lanes * rows, lanes), F32),
            pltpu.VMEM(((frames + 1) * chunks * halves + 2 * tokens, lanes), F32),
        ],
        compiler_params=params(),
        cost_estimate=pl.CostEstimate(
            flops=cache.size, bytes_accessed=6 * cache.size, transcendentals=0
        ),
        name="prepare",
    )(span_index, facts, cache, noisy, latents)


def shift_down(array):
    moved_rows = pltpu.roll(array, 1, axis=0)
    rows = lax.broadcasted_iota(jnp.int32, array.shape, 0)
    return jnp.where(rows == 0, 0.0, moved_rows)


def shift_up(array):
    count = array.shape[0]
    moved_rows = pltpu.roll(array, count - 1, axis=0)
    rows = lax.broadcasted_iota(jnp.int32, array.shape, 0)
    return jnp.where(rows == count - 1, 0.0, moved_rows)


def tap_sum(line, rows, steps, weight):
    lines = []
    for b in range(2):
        for r in rows:
            lines.append(
                jnp.concatenate(
                    [line(b + w, r + h - 1) for h in steps for w in range(3)], axis=1
                )
            )
    total = dot_last(jnp.concatenate(lines, axis=0), weight)
    half = total.shape[0] // 2
    return jnp.concatenate([total[:half], total[half:]], axis=1)


def middle_kernel(own_ref, weight_hbm, out_ref, rim_ref, weight_ref, sems):
    rows = own_ref.shape[1]
    depth = weight_ref.shape[2]
    third = depth // 3
    head = lax.axis_index("head")
    copies = [
        pltpu.make_async_copy(
            weight_hbm.at[:, pl.ds(t * depth, depth)], weight_ref.at[t], sems.at[t]
        )
        for t in range(2)
    ]
    for copy in copies:
        copy.start()

    def line(n, r):
        return own_ref[n, r]

    def contribute(f, t):
        weight = weight_ref[t]
        inner = tap_sum(line, range(1, rows - 1), range(3), weight).astype(BF)
        out_ref[f] = inner.reshape(out_ref.shape[1:])
        rim_ref[f, 0] = tap_sum(line, (0,), (1, 2), weight[:, third:])
        rim_ref[f, 1] = tap_sum(line, (rows - 1,), (0, 1), weight[:, : 2 * third])

    copies[0].wait()
    contribute(head, 0)
    copies[1].wait()

    @pl.when(head == 0)
    def _():
        out_ref[1] = jnp.zeros(out_ref.shape[1:], BF)

    @pl.when(head != 0)
    def _():
        contribute(0, 1)


def middles(own, weight):
    _, rows, cols, channels = own.shape
    out, height = weight.shape
    return pl.pallas_call(
        middle_kernel,
        in_specs=[whole(), far_spec()],
        out_specs=[whole(), whole()],
        out_shape=[
            jax.ShapeDtypeStruct((2, rows - 2, cols, 2 * out), BF),
            jax.ShapeDtypeStruct((2, 2, cols, 2 * out), F32),
        ],
        scratch_shapes=[
            pltpu.VMEM((2, out, height // 3), BF),
            pltpu.SemaphoreType.DMA((2,)),
        ],
        compiler_params=params(),
        cost_estimate=pl.CostEstimate(
            flops=2 * 2 * 2 * 3 * cols * 9 * channels * out,
            bytes_accessed=2 * (own.size + weight.size),
            transcendentals=0,
        ),
        name="middle",
    )(own, far(weight))


def edge_kernel(rim_ref, above_ref, below_ref, weight_hbm, out_ref, var, weight_ref, sems):
    _, _, cols, channels = var.shape
    depth = weight_ref.shape[3]
    head = lax.axis_index("head")
    copies = [
        [
            pltpu.make_async_copy(
                weight_hbm.at[:, pl.ds((t * 3 + 2 * n) * depth, depth)],
                weight_ref.at[t, n],
                sems.at[t * 2 + n],
            )
            for n in range(2)
        ]
        for t in range(2)
    ]
    for pair in copies:
        for copy in pair:
            copy.start()

    for n, far_rim in enumerate((above_ref, below_ref)):
        even, odd = far_rim[:cols], far_rim[cols : 2 * cols]
        var[n, 0] = shift_down(odd.astype(F32)).astype(BF)
        var[n, 1] = even
        var[n, 2] = odd
        var[n, 3] = shift_up(even.astype(F32)).astype(BF)

    def contribute(f, t):
        for n in range(2):
            late = tap_sum(lambda v, r: var[n, v], (0,), (0,), weight_ref[t, n])
            out_ref[f, n] = (rim_ref[f, n] + late).astype(BF)

    for copy in copies[0]:
        copy.wait()
    contribute(head, 0)
    for copy in copies[1]:
        copy.wait()

    @pl.when(head == 0)
    def _():
        out_ref[1] = jnp.zeros(out_ref.shape[1:], BF)

    @pl.when(head != 0)
    def _():
        contribute(0, 1)


def edges(rim, above, below, weight, channels):
    _, _, cols, width = rim.shape
    out, height = weight.shape
    return pl.pallas_call(
        edge_kernel,
        in_specs=[whole(), whole(), whole(), far_spec()],
        out_specs=whole(),
        out_shape=jax.ShapeDtypeStruct(rim.shape, BF),
        scratch_shapes=[
            pltpu.VMEM((2, 4, cols, channels), BF),
            pltpu.VMEM((2, 2, out, height // 9), BF),
            pltpu.SemaphoreType.DMA((4,)),
        ],
        compiler_params=params(),
        cost_estimate=pl.CostEstimate(
            flops=2 * 2 * 2 * 2 * cols * 3 * channels * out,
            bytes_accessed=2 * (above.size + weight.size),
            transcendentals=0,
        ),
        name="edge",
    )(rim, above, below, far(weight))


def mix_kernel(weight_ref, out_ref):
    channels = weight_ref.shape[1] // 9

    def tap(h, w):
        start = (h * 3 + w) * channels
        return weight_ref[:, start : start + channels].astype(F32)

    lines = {}
    for w in range(3):
        top, middle, bottom = tap(0, w), tap(1, w), tap(2, w)
        lines[0, 0, w] = top
        lines[0, 1, w] = middle + bottom
        lines[1, 0, w] = top + middle
        lines[1, 1, w] = bottom
    for a in range(2):
        for u in range(2):
            left, centre, right = [lines[a, u, w] for w in range(3)]
            mixed = ((left, centre + right), (left + centre, right))
            for b in range(2):
                for v in range(2):
                    start = (u * 2 + v) * channels
                    out_ref[0, a * 2 + b, :, start : start + channels] = mixed[b][v].astype(BF)


def mix(weight):
    out, height = weight.shape
    third = height // 3
    shape = (3, 4, out, third // 9 * 4)
    return pl.pallas_call(
        mix_kernel,
        grid=(3,),
        in_specs=[pl.BlockSpec((out, third), lambda t: (0, t))],
        out_specs=pl.BlockSpec((1,) + shape[1:], lambda t: (t, 0, 0, 0)),
        out_shape=jax.ShapeDtypeStruct(shape, BF),
        compiler_params=params(1),
        cost_estimate=pl.CostEstimate(
            flops=4 * weight.size, bytes_accessed=6 * weight.size, transcendentals=0
        ),
        name="mix",
    )(weight)


def spread(source_ref, var):
    frames, coarse = source_ref.shape[:2]
    for f in range(frames):
        for r in range(coarse):
            plain = source_ref[f, r]
            wide = plain.astype(F32)
            var[0, f, r] = shift_down(wide).astype(BF)
            var[1, f, r] = plain
            var[2, f, r] = shift_up(wide).astype(BF)


def taps(var, frames, a, b):
    coarse = var.shape[2]
    lines = []
    for frame in frames:
        for r in range(coarse - 2):
            lines.append(
                jnp.concatenate(
                    [var[b + v, frame, r + a + u] for u in range(2) for v in range(2)], axis=1
                )
            )
    return jnp.concatenate(lines, axis=0)


def own_kernel(source_ref, old_ref, new_ref, out_ref, var):
    step = pl.program_id(0)
    a = step // 2
    b = step % 2

    @pl.when(step == 0)
    def _():
        spread(source_ref, var)

    both = dot_last(taps(var, (0, 1), a, b), new_ref[0, 0])
    more = dot_last(taps(var, (0,), a, b), old_ref[0, 0])
    height = more.shape[0]
    shape = out_ref.shape[2:]
    out_ref[0, 0] = both[:height].reshape(shape)
    out_ref[0, 1] = (both[height:] + more).reshape(shape)


def own_part(activated, mixed):
    frames, coarse, cols, channels = activated.shape
    _, parities, width, depth = mixed.shape
    block = (1, 1, width, depth)
    shape = (parities, frames, coarse - 2, cols, width)
    return pl.pallas_call(
        own_kernel,
        grid=(parities,),
        in_specs=[
            pl.BlockSpec(activated.shape, lambda i: (0, 0, 0, 0)),
            pl.BlockSpec(block, lambda i: (1, i, 0, 0)),
            pl.BlockSpec(block, lambda i: (2, i, 0, 0)),
        ],
        out_specs=pl.BlockSpec((1,) + shape[1:], lambda i: (i, 0, 0, 0, 0)),
        out_shape=jax.ShapeDtypeStruct(shape, F32),
        scratch_shapes=[pltpu.VMEM((3, frames, coarse, cols, channels), BF)],
        compiler_params=params(1),
        cost_estimate=pl.CostEstimate(
            flops=2 * 3 * 2 * cols * depth * width * parities,
            bytes_accessed=2 * (activated.size + 2 * parities * width * depth),
            transcendentals=0,
        ),
        name="own_part",
    )(activated, mixed, mixed)


def prior_kernel(source_ref, middle_ref, edge_ref, own_ref, old_ref, new_ref, out_ref, var, total_ref, scr):
    parities, frames, coarse_rows, cols, width = total_ref.shape
    head = lax.axis_index("head")
    step = pl.program_id(0)
    a = step // 2
    b = step % 2

    @pl.when(head == 0)
    def _():
        total_ref[step] = own_ref[0]

    @pl.when(head != 0)
    def _():
        @pl.when(step == 0)
        def _():
            spread(source_ref, var)

        both = dot_last(taps(var, (0, 1), a, b), old_ref[0, 0])
        more = dot_last(taps(var, (1,), a, b), new_ref[0, 0])
        height = more.shape[0]
        shape = total_ref.shape[2:]
        total_ref[step, 0] = own_ref[0, 0] + (both[:height] + more).reshape(shape)
        total_ref[step, 1] = own_ref[0, 1] + both[height:].reshape(shape)

    @pl.when(step == parities - 1)
    def _():
        fine = 2 * coarse_rows
        pieces = 2 * width // 128
        keep = jnp.where(head == 0, 1.0, 0.0)
        for f in range(frames):
            for row in range(fine):
                side = (row % 2) * 2
                sides = [total_ref[side + n, f, row // 2] for n in range(2)]
                line = jnp.concatenate(sides, axis=1)
                if row in (0, fine - 1):
                    mine = edge_ref[f, min(row, 1)]
                else:
                    mine = middle_ref[f, row - 1]
                extra = mine.astype(F32) + source_ref[f, row].astype(F32)
                line = line + keep * extra
                for q in range(pieces):
                    scr[pl.ds(q * fine + row, cols, stride=pieces * fine), :] = line[
                        :, q * 128 : (q + 1) * 128
                    ]

            for at in range(out_ref.shape[1]):
                out_ref[f, at] = scr[at * fine : (at + 1) * fine, :].astype(BF)


def prior_part(received, middle, edge, own_sum, mixed):
    frames, coarse, cols, channels = received.shape
    _, parities, width, depth = mixed.shape
    fine = 2 * (coarse - 2)
    tiles = cols * 2 * width // 128
    block = (1, 1, width, depth)
    out = pl.pallas_call(
        prior_kernel,
        grid=(parities,),
        in_specs=[
            pl.BlockSpec(received.shape, lambda i: (0, 0, 0, 0)),
            pl.BlockSpec(middle.shape, lambda i: (0, 0, 0, 0)),
            pl.BlockSpec(edge.shape, lambda i: (0, 0, 0, 0)),
            pl.BlockSpec((1,) + own_sum.shape[1:], lambda i: (i, 0, 0, 0, 0)),
            pl.BlockSpec(block, lambda i: (0, i, 0, 0)),
            pl.BlockSpec(block, lambda i: (1, i, 0, 0)),
        ],
        out_specs=pl.BlockSpec((frames, tiles, fine, 128), lambda i: (0, 0, 0, 0)),
        out_shape=jax.ShapeDtypeStruct((frames, tiles, fine, 128), BF),
        scratch_shapes=[
            pltpu.VMEM((3, frames, coarse, cols, channels), BF),
            pltpu.VMEM(own_sum.shape, F32),
            pltpu.VMEM((tiles * fine, 128), F32),
        ],
        compiler_params=params(1),
        cost_estimate=pl.CostEstimate(
            flops=2 * 3 * 2 * cols * depth * width * parities,
            bytes_accessed=2 * (received.size + 2 * parities * width * depth),
            transcendentals=0,
        ),
        name="prior_part",
    )(received, middle, edge, own_sum, mixed, mixed)
    return out.transpose(0, 2, 1, 3).reshape(frames, fine, tiles * 128)


def latent_kernel(step_ref, parts_ref, own_ref, above_ref, below_ref, clean_ref, send_ref, out_ref, scr):
    sources, three, unit, lanes = parts_ref.shape
    cols = own_ref.shape[0]
    frames, chunks, halves = out_ref.shape[:3]
    groups = frames * halves
    group = lanes // groups
    features = sources * 128
    fraction = 1.0 - step_ref[0].astype(F32) / NSTEPS
    fraction = jnp.full((1, lanes), fraction, F32)
    level = SHIFT_FACTOR * fraction / (1.0 + (SHIFT_FACTOR - 1.0) * fraction)
    total = parts_ref[0].astype(F32)
    for source in range(1, sources):
        total = total + parts_ref[source].astype(F32)
    half = lax.broadcasted_iota(jnp.int32, (cols, lanes), 1) < lanes // 2
    first_group = lax.axis_index("head") == 0
    for k, small_ref in ((0, above_ref), (1, own_ref), (2, below_ref)):
        small = small_ref[...] if k == 1 else small_ref[small_ref.shape[0] - cols :]
        sums = jnp.transpose(total[k, cols:unit])[:cols]
        scale = lax.rsqrt(sums / features + NORM_EPSILON)
        scale = jnp.where(half, scale[:, 0:1], scale[:, 1:2])
        velocity = total[k, :cols] * scale
        clean = (small[:, :lanes].astype(F32) - level * velocity).astype(BF)
        clean_ref[k] = clean
        if k == 1:
            scr[:cols, :] = clean.astype(F32)

        @pl.when(first_group)
        def _():
            send_ref[k] = clean

        @pl.when(jnp.logical_not(first_group))
        def _():
            send_ref[k] = small[:, lanes : 2 * lanes]

    parts = [scr[pl.ds(m, chunks, stride=groups), :] for m in range(groups)]
    for g in range(groups):
        total_line = None
        for m, part in enumerate(parts):
            term = jnp.where(lane_groups(part, group) == m, moved(part, group * (m - g)), 0.0)
            total_line = term if total_line is None else total_line + term
        f, a = g // halves, g % halves
        scr[pl.ds(cols + f * chunks * halves + a, chunks, stride=halves), :] = total_line
    for f in range(frames):
        for i in range(chunks):
            at = cols + (f * chunks + i) * halves
            out_ref[f, i] = scr[at : at + halves, :].astype(BF)


def latent(step_index, parts, own, above, below, frames, halves, chunks):
    sources, three, unit, lanes = parts.shape
    cols = own.shape[0]
    shape = jax.ShapeDtypeStruct((three, cols, lanes), BF)
    return pl.pallas_call(
        latent_kernel,
        in_specs=[smem()] + [whole()] * 4,
        out_specs=[whole(), whole(), whole()],
        out_shape=[shape, shape, jax.ShapeDtypeStruct((frames, chunks, halves, 128), BF)],
        scratch_shapes=[pltpu.VMEM((cols + frames * chunks * halves, lanes), F32)],
        compiler_params=params(0, 8),
        cost_estimate=pl.CostEstimate(
            flops=2 * parts.size, bytes_accessed=2 * parts.size, transcendentals=0
        ),
        name="latent",
    )(step_index, parts, own, above, below)


def first_kernel(
    clean_ref, received_ref, own_ref, above_ref, below_ref, weight_ref, gain_ref, middle_ref, edge_ref, act_ref, send_ref, left, padded, scr
):
    three, cols, lanes = clean_ref.shape
    frames, coarse = act_ref.shape[:2]
    channels = act_ref.shape[3]
    group = lanes // 4
    slot = lanes // 2
    part = group // 2
    head = lax.axis_index("head")
    three_taps = weight_ref.shape[0] // 9
    gap = jnp.zeros((slot - three_taps, channels), BF)
    for n in range(9):
        padded[n * slot : n * slot + three_taps, :] = weight_ref[
            n * three_taps : (n + 1) * three_taps, :
        ]
        padded[n * slot + three_taps : (n + 1) * slot, :] = gap
    padded[9 * slot :, :] = jnp.zeros((slot, channels), BF)
    gains = gain_ref[...].astype(F32)
    gain = jnp.concatenate([gains[q : q + 1] for q in range(gains.shape[0])], axis=1)
    cached_old = jnp.concatenate(
        [
            above_ref[above_ref.shape[0] - cols :, lanes : 2 * lanes].astype(F32),
            own_ref[:, lanes : 2 * lanes].astype(F32),
            below_ref[below_ref.shape[0] - cols :, lanes : 2 * lanes].astype(F32),
        ],
        axis=0,
    )
    clean = jnp.concatenate([clean_ref[k].astype(F32) for k in range(three)], axis=0)
    arrived = jnp.concatenate([received_ref[k].astype(F32) for k in range(three)], axis=0)
    lane = lax.broadcasted_iota(jnp.int32, clean.shape, 1)
    line = lax.broadcasted_iota(jnp.int32, clean.shape, 0)
    at = lax.rem(line, cols)
    older = jnp.where(
        head == 0, jnp.where(lane < lanes // 2, cached_old, arrived), arrived
    )
    pieces = {}
    for source, x in enumerate((older, clean)):
        height = x.shape[0]
        before = jnp.where(at == 0, 0.0, pltpu.roll(x, 1, axis=0))
        after = jnp.where(at == cols - 1, 0.0, pltpu.roll(x, height - 1, axis=0))
        for f in range(2):
            for a in range(2):
                off = f * (lanes // 2) + a * group
                for side in range(2):
                    base = side * slot

                    low = lane - base
                    even = jnp.where(
                        (low >= 0) & (low < part),
                        moved(before, base - off - part),
                        jnp.where(
                            (low >= part) & (low < 3 * part), moved(x, base + part - off), 0.0
                        ),
                    )
                    odd = jnp.where(
                        (low >= 0) & (low < 2 * part),
                        moved(x, base - off),
                        jnp.where(
                            (low >= 2 * part) & (low < 3 * part),
                            moved(after, base + 2 * part - off),
                            0.0,
                        ),
                    )
                    pieces[source * 2 + f, a, side, 0] = even
                    pieces[source * 2 + f, a, side, 1] = odd

    def piece(p, fo, ro, n):
        frame = fo + n // 3
        row = ro + n % 3
        k = row // 2
        return pieces[frame, row % 2, n % 2, p][k * cols : (k + 1) * cols]

    for p in range(2):
        for fo in range(frames):
            for ro in range(coarse):
                start = ((p * frames + fo) * coarse + ro) * cols
                for j in range(5):
                    block = piece(p, fo, ro, 2 * j)
                    if 2 * j + 1 < 9:
                        block = block + piece(p, fo, ro, 2 * j + 1)
                    left[start : start + cols, j * lanes : (j + 1) * lanes] = block.astype(BF)

    feat = dot(left[...], padded[...])
    mean_square = jnp.mean(feat * feat, axis=-1, keepdims=True)
    normed = feat * lax.rsqrt(mean_square + NORM_EPSILON) * gain
    active = normed / (1.0 + jnp.exp(-normed))
    slab = lax.axis_index("seq")
    last = lax.axis_size("seq") - 1
    keep_first = jnp.where(slab == 0, 0.0, 1.0)
    keep_last = jnp.where(slab == last, 0.0, 1.0)
    for p in range(2):
        for fo in range(frames):
            for ro in range(coarse):
                start = ((p * frames + fo) * coarse + ro) * cols
                block = active[start : start + cols]
                if ro == 0:
                    block = block * keep_first
                if ro == coarse - 1:
                    block = block * keep_last
                to = (fo * coarse + ro) * 2 * cols + p
                for q in range(channels // 128):
                    scr[q, pl.ds(to, cols, stride=2), :] = block[:, q * 128 : (q + 1) * 128]
    for fo in range(frames):
        for ro in range(coarse):
            to = (fo * coarse + ro) * 2 * cols
            for q in range(channels // 128):
                act_ref[fo, ro, :, q * 128 : (q + 1) * 128] = scr[q, to : to + 2 * cols, :].astype(BF)

    @pl.when(head == 0)
    def _():
        send_ref[...] = act_ref[...]

    @pl.when(head != 0)
    def _():
        for fo in range(frames):
            send_ref[fo, 0] = edge_ref[fo, 0]
            send_ref[fo, coarse - 1] = edge_ref[fo, 1]
            for ro in range(1, coarse - 1):
                send_ref[fo, ro] = middle_ref[fo, ro - 1]


def first(clean, received, own, above, below, weight, gain, middle, edge):
    three, cols, lanes = clean.shape
    frames, inner, wide, channels = middle.shape
    coarse = inner + 2
    shape = jax.ShapeDtypeStruct((frames, coarse, wide, channels), BF)
    height = frames * coarse * wide
    return pl.pallas_call(
        first_kernel,
        in_specs=[whole()] * 9,
        out_specs=[whole(), whole()],
        out_shape=[shape, shape],
        scratch_shapes=[
            pltpu.VMEM((height, 5 * lanes), BF),
            pltpu.VMEM((5 * lanes, channels), BF),
            pltpu.VMEM((channels // 128, height, 128), F32),
        ],
        compiler_params=params(),
        cost_estimate=pl.CostEstimate(
            flops=2 * height * weight.size, bytes_accessed=8 * middle.size, transcendentals=height * channels
        ),
        name="first",
    )(clean, received, own, above, below, weight, gain, middle, edge)


def swapped(array, axis):
    return lax.ppermute(array, axis, [(0, 1), (1, 0)])


def body(
    queries,
    keys,
    values,
    final_gain,
    out_weight,
    noisy_latent,
    step_index,
    span_index,
    cache_flags,
    latent_cache,
    feature_cache,
    first_weight,
    first_gain,
    second_weight,
):
    channels = first_weight.shape[1]
    slabs = lax.axis_size("seq")
    frames, halves, width = noisy_latent.shape
    second = second_weight.T

    sent, facts, cache, noisy, latents = attention(
        queries,
        keys,
        values,
        final_gain,
        out_weight,
        cache_flags,
        feature_cache,
        noisy_latent,
        latent_cache,
    )
    parts = lax.all_to_all(sent, "seq", 0, 0, tiled=True)
    own_frame, up, down, small = prepare(
        span_index, facts, cache, noisy, latents, channels
    )
    above = lax.ppermute(down, "seq", [(i, i + 1) for i in range(slabs - 1)])
    below = lax.ppermute(up, "seq", [(i + 1, i) for i in range(slabs - 1)])
    middle, rim = middles(own_frame, second)
    above, below, middle = lax.optimization_barrier((above, below, middle))

    clean, send, out = latent(step_index, parts, small, above, below, frames, halves, width // 128)
    edge = edges(rim, above, below, second, channels)
    received = swapped(send, "head")
    activated, send = first(
        clean, received, small, above, below, first_weight, first_gain.reshape(-1, 128), middle, edge
    )
    arrived = swapped(send, "head")
    mixed = mix(second)
    own_sum = own_part(activated, mixed)
    decoded = prior_part(arrived, middle, edge, own_sum, mixed)
    return (out.transpose(0, 2, 1, 3).reshape(frames, halves, width), decoded)


def solution(mesh):
    in_specs = (
        P(("grp", "head"), None, None, "seq"),
        P("grp", None, None, "seq"),
        P("grp", None, None, "seq"),
        P(),
        P(),
        P(("grp", "head"), "seq", None),
        P("grp"),
        P("grp"),
        P("grp", None, None),
        P("grp", "head", "seq", None),
        P("grp", "head", "seq", None),
        P(),
        P(),
        P(),
    )
    out_specs = (P(("grp", "head"), "seq", None), P(("grp", "head"), "seq", None))
    return jax.shard_map(body, mesh=mesh, in_specs=in_specs, out_specs=out_specs, check_vma=False)
```

```python
import jax
import jax.numpy as jnp
from jax import lax
from jax.experimental import pallas as pl
from jax.experimental.pallas import tpu as pltpu
from jax.sharding import PartitionSpec as P

NSTEPS = 16
CSLOTS = 2
SHIFT_FACTOR = 5.0
NORM_EPSILON = 1e-06
BF = jnp.bfloat16
F32 = jnp.float32
LAST = (((1,), (1,)), ((), ()))


def params(dims=0, mib=12):
    semantics = ("arbitrary",) * dims if dims else None
    return pltpu.CompilerParams(dimension_semantics=semantics, vmem_limit_bytes=mib << 20)


def dot(left, right):
    return jnp.dot(left, right, preferred_element_type=F32)


def dot_last(left, right):
    return lax.dot_general(left, right, LAST, preferred_element_type=F32)


def smem():
    return pl.BlockSpec(memory_space=pltpu.SMEM)


def far(array):
    return pltpu.with_memory_space_constraint(array, pltpu.HBM)


def far_spec():
    return pl.BlockSpec(memory_space=pltpu.HBM)


def whole():
    return pl.BlockSpec(memory_space=pltpu.VMEM)


def attention_kernel(
    flags_hbm,
    q_hbm,
    k_hbm,
    v_hbm,
    gain_hbm,
    weight_hbm,
    cache_hbm,
    noisy_hbm,
    latent_hbm,
    out_ref,
    facts_ref,
    cache_ref,
    noisy_ref,
    latent_ref,
    flags_ref,
    q_ref,
    k_ref,
    v_ref,
    gain_ref,
    weight_ref,
    sems,
    *,
    cols,
    rows,
):
    slab = lax.axis_index("seq")
    head = lax.axis_index("head")
    frames, query_count, head_size = q_ref.shape
    rows_total = query_count // cols
    count = [0]

    def load(source, target):
        copy = pltpu.make_async_copy(source, target, sems.at[count[0]])
        count[0] += 1
        copy.start()
        return copy

    key_copies = [load(q_hbm, q_ref), load(k_hbm, k_ref)]
    value_copies = [load(v_hbm, v_ref), load(gain_hbm, gain_ref), load(weight_hbm, weight_ref)]
    later = [
        load(flags_hbm, flags_ref),
        load(cache_hbm, cache_ref),
        load(latent_hbm, latent_ref),
        load(noisy_hbm, noisy_ref),
    ]
    edge = jnp.zeros(out_ref.shape[2:], BF)
    out_ref[0, 0] = edge
    out_ref[rows_total - 1, 2] = edge
    for copy in key_copies:
        copy.wait()
    first_scores = [dot_last(q_ref[f, : rows * cols, :], k_ref[...]) for f in range(frames)]
    for copy in value_copies:
        copy.wait()

    scale = 1.4426950408889634 / head_size**0.5
    keys = k_ref[...]
    values = jnp.concatenate([v_ref[...], jnp.ones_like(v_ref[...])], axis=1)
    gains = gain_ref[...].astype(F32)
    chosen = lax.broadcasted_iota(jnp.int32, gains.shape, 0) == slab
    gain = jnp.sum(jnp.where(chosen, gains, 0.0), axis=0, keepdims=True)
    start = pl.multiple_of(slab * head_size, head_size)
    weight = weight_ref[:, pl.ds(start, head_size)]
    none = jnp.zeros_like(weight)
    line_of = lax.broadcasted_iota(jnp.int32, (8, head_size), 0)

    def block(step):
        total = None
        squares = []
        for f in range(frames):
            at = step * (rows * cols)
            if not isinstance(step, int):
                at = pl.multiple_of(at, 16)
            if isinstance(step, int) and step == 0:
                scores = first_scores[f]
            else:
                scores = dot_last(q_ref[f, pl.ds(at, rows * cols), :], keys)
            row_max = jnp.max(scores, axis=1, keepdims=True)
            weights = jnp.exp2((scores - row_max) * scale).astype(BF)
            blended = dot(weights, values)
            attended = (blended[:, :head_size] / blended[:, head_size:]).astype(BF).astype(F32)
            side = [none] * frames
            side[f] = weight
            part = dot_last((attended * gain).astype(BF), jnp.concatenate(side, axis=0))
            total = part if total is None else total + part
            squares.append(attended * attended)
        for r in range(rows):
            sums = None
            for f in range(frames):
                piece = squares[f][r * cols : (r + 1) * cols].astype(BF)
                line = dot_last((line_of == f).astype(F32).astype(BF), piece)
                sums = line if sums is None else sums + line
            lanes = total.shape[1]
            sums = jnp.concatenate([sums, jnp.zeros((8, lanes - cols), F32)], axis=1)
            unit = jnp.concatenate([total[r * cols : (r + 1) * cols], sums], axis=0).astype(BF)
            row = step * rows + r
            out_ref[row, 1] = unit
            if isinstance(step, int):
                if row + 1 < rows_total:
                    out_ref[row + 1, 0] = unit
                if row > 0:
                    out_ref[row - 1, 2] = unit
            else:

                @pl.when(row + 1 < rows_total)
                def _():
                    out_ref[jnp.minimum(row + 1, rows_total - 1), 0] = unit

                @pl.when(row > 0)
                def _():
                    out_ref[jnp.maximum(row - 1, 0), 2] = unit

    steps = rows_total // rows
    block(0)
    if steps <= 2:
        for step in range(1, steps):
            block(step)
    else:

        def one(step, carry):
            block(step)
            return carry

        lax.fori_loop(1, steps, one, 0)

    for copy in later:
        copy.wait()
    slots, _, coarse, _ = latent_ref.shape
    for slot in range(slots):
        for r in range(coarse):
            flag = flags_ref[slot, head, slab * coarse + r].astype(F32)
            at = slot * coarse + r
            facts_ref[at : at + 1, :] = jnp.full((1, 128), flag, F32)


def attention(
    queries,
    keys,
    values,
    final_gain,
    out_weight,
    cache_flags,
    feature_cache,
    noisy_latent,
    latent_cache,
):
    frames, rows_total, cols, head_size = queries.shape
    q = queries.reshape(frames, rows_total * cols, head_size)
    k = keys.reshape(-1, head_size)
    v = values.reshape(-1, head_size)
    gains = final_gain.reshape(-1, head_size)
    weight = out_weight.T
    rows = 4 if rows_total % 4 == 0 else rows_total
    lanes = frames * weight.shape[0]
    unit = cols + 8
    cache = tiled(feature_cache[:, 0])
    noisy = tiled(noisy_latent)
    latents = tiled(latent_cache[:, 0])

    def kernel(*refs):
        attention_kernel(*refs, cols=cols, rows=rows)

    count = frames * rows_total * cols
    shapes = [
        ((rows_total, 3, unit, lanes), BF),
        ((8, 128), F32),
        (cache.shape, BF),
        (noisy.shape, BF),
        (latents.shape, BF),
    ]
    return pl.pallas_call(
        kernel,
        in_specs=[far_spec()] * 9,
        out_specs=[whole()] * len(shapes),
        out_shape=[pltpu.VMEM(shape, kind) for shape, kind in shapes],
        scratch_shapes=[
            pltpu.SMEM(cache_flags.shape, jnp.int32),
            pltpu.VMEM(q.shape, BF),
            pltpu.VMEM(k.shape, BF),
            pltpu.VMEM(v.shape, BF),
            pltpu.VMEM(gains.shape, BF),
            pltpu.VMEM(weight.shape, BF),
            pltpu.SemaphoreType.DMA((9,)),
        ],
        compiler_params=params(0, 40),
        cost_estimate=pl.CostEstimate(
            flops=6 * count * k.shape[0] * head_size,
            bytes_accessed=2 * (q.size + k.size + v.size),
            transcendentals=count * k.shape[0],
        ),
        name="attention",
    )(
        *[
            far(array)
            for array in (
                cache_flags,
                q,
                k,
                v,
                gains,
                weight,
                cache,
                noisy,
                latents,
            )
        ]
    )


def lane_groups(array, group):
    return lax.broadcasted_iota(jnp.int32, array.shape, 1) // group


def moved(array, shift):
    lanes = array.shape[1]
    shift = shift % lanes
    return pltpu.roll(array, shift, axis=1) if shift else array


def prepare_kernel(span_ref, facts_ref, cache_ref, noisy_ref, latent_ref, own_ref, up_ref, down_ref, small_ref, scr, lat):
    _, tiles, rows, lanes = cache_ref.shape
    cols, channels = own_ref.shape[2:]
    pieces = channels // lanes
    coarse = rows // 2
    slot = lax.rem(span_ref[0], CSLOTS)
    flags = [facts_ref[pl.ds(slot * coarse + r, 1), :] for r in range(coarse)]
    whole_column = 2 * pieces * rows

    frames, chunks, halves = noisy_ref.shape[:3]
    groups = frames * halves
    group = lanes // groups
    for f in range(frames + 1):
        for i in range(chunks):
            tile = latent_ref[slot, i] if f == frames else noisy_ref[f, i]
            lat[pl.ds((f * chunks + i) * halves, halves), :] = tile.astype(F32)
    lines = [
        [lat[pl.ds(f * chunks * halves + a, chunks, stride=halves), :] for a in range(halves)]
        for f in range(frames + 1)
    ]
    noisy = [lines[f][a] for f in range(frames) for a in range(halves)]
    old = [lines[frames][a] * flags[a] for f in range(frames) for a in range(halves)]
    base = (frames + 1) * chunks * halves
    tokens = chunks * groups
    for n, parts in enumerate((noisy, old)):
        at = base + n * tokens
        for m in range(groups):
            total = None
            for g, part in enumerate(parts):
                term = jnp.where(lane_groups(part, group) == g, moved(part, group * (g - m)), 0.0)
                total = term if total is None else total + term
            lat[pl.ds(at + m, chunks, stride=groups), :] = total
        block = lat[at : at + tokens, :].astype(BF)
        small_ref[:, n * lanes : (n + 1) * lanes] = block
        up_ref[2 * cols :, n * lanes : (n + 1) * lanes] = block
        down_ref[2 * cols :, n * lanes : (n + 1) * lanes] = block
    rest = jnp.zeros((tokens, channels - 2 * lanes), BF)
    up_ref[2 * cols :, 2 * lanes :] = rest
    down_ref[2 * cols :, 2 * lanes :] = rest

    pad = jnp.zeros((whole_column, lanes), F32)
    scr[:whole_column, :] = pad
    scr[whole_column + tiles * rows :, :] = pad

    def unpack(i, carry):
        for n in range(16):
            at = i * 16 + n
            to = pl.multiple_of(whole_column + at * rows, rows)
            scr[pl.ds(to, rows), :] = cache_ref[slot, at].astype(F32)
        return carry

    lax.fori_loop(0, tiles // 16, unpack, 0)
    for r in range(rows):
        for n in range(4):
            for q in range(pieces):
                column = whole_column * ((n + 1) // 2) + ((n + 1) % 2) * pieces * rows
                start = column + q * rows + r
                piece = scr[pl.ds(start, cols, stride=whole_column), :]
                piece = (piece * flags[r // 2]).astype(BF)
                own_ref[n, r, :, q * lanes : (q + 1) * lanes] = piece
                if n in (1, 2):
                    to = slice((n - 1) * cols, n * cols)
                    if r == 0:
                        up_ref[to, q * lanes : (q + 1) * lanes] = piece
                    if r == rows - 1:
                        down_ref[to, q * lanes : (q + 1) * lanes] = piece


def tiled(array):
    *lead, rows, width = array.shape
    count = len(lead)
    view = array.reshape(*lead, rows, width // 128, 128)
    return view.transpose(*range(count), count + 1, count, count + 2)


def prepare(span_index, facts, cache, noisy, latents, channels):
    _, tiles, rows, lanes = cache.shape
    cols = tiles * lanes // channels // 2
    frames, chunks, halves = noisy.shape[:3]
    tokens = chunks * frames * halves
    halo = 2 * cols + tokens
    return pl.pallas_call(
        prepare_kernel,
        in_specs=[smem()] + [whole()] * 4,
        out_specs=[whole()] * 4,
        out_shape=[
            jax.ShapeDtypeStruct((4, rows, cols, channels), BF),
            jax.ShapeDtypeStruct((halo, channels), BF),
            jax.ShapeDtypeStruct((halo, channels), BF),
            jax.ShapeDtypeStruct((tokens, 256), BF),
        ],
        scratch_shapes=[
            pltpu.VMEM((tiles * rows + 4 * channels // lanes * rows, lanes), F32),
            pltpu.VMEM(((frames + 1) * chunks * halves + 2 * tokens, lanes), F32),
        ],
        compiler_params=params(),
        cost_estimate=pl.CostEstimate(
            flops=cache.size, bytes_accessed=6 * cache.size, transcendentals=0
        ),
        name="prepare",
    )(span_index, facts, cache, noisy, latents)


def shift_down(array):
    moved_rows = pltpu.roll(array, 1, axis=0)
    rows = lax.broadcasted_iota(jnp.int32, array.shape, 0)
    return jnp.where(rows == 0, 0.0, moved_rows)


def shift_up(array):
    count = array.shape[0]
    moved_rows = pltpu.roll(array, count - 1, axis=0)
    rows = lax.broadcasted_iota(jnp.int32, array.shape, 0)
    return jnp.where(rows == count - 1, 0.0, moved_rows)


def tap_sum(line, rows, steps, weight):
    lines = []
    for b in range(2):
        for r in rows:
            lines.append(
                jnp.concatenate(
                    [line(b + w, r + h - 1) for h in steps for w in range(3)], axis=1
                )
            )
    total = dot_last(jnp.concatenate(lines, axis=0), weight)
    half = total.shape[0] // 2
    return jnp.concatenate([total[:half], total[half:]], axis=1)


def middle_kernel(own_ref, weight_hbm, out_ref, rim_ref, weight_ref, sems):
    rows = own_ref.shape[1]
    depth = weight_ref.shape[2]
    third = depth // 3
    head = lax.axis_index("head")
    copies = [
        pltpu.make_async_copy(
            weight_hbm.at[:, pl.ds(t * depth, depth)], weight_ref.at[t], sems.at[t]
        )
        for t in range(2)
    ]
    for copy in copies:
        copy.start()

    def line(n, r):
        return own_ref[n, r]

    def contribute(f, t):
        weight = weight_ref[t]
        inner = tap_sum(line, range(1, rows - 1), range(3), weight).astype(BF)
        out_ref[f] = inner.reshape(out_ref.shape[1:])
        rim_ref[f, 0] = tap_sum(line, (0,), (1, 2), weight[:, third:])
        rim_ref[f, 1] = tap_sum(line, (rows - 1,), (0, 1), weight[:, : 2 * third])

    copies[0].wait()
    contribute(head, 0)
    copies[1].wait()

    @pl.when(head == 0)
    def _():
        out_ref[1] = jnp.zeros(out_ref.shape[1:], BF)

    @pl.when(head != 0)
    def _():
        contribute(0, 1)


def middles(own, weight):
    _, rows, cols, channels = own.shape
    out, height = weight.shape
    return pl.pallas_call(
        middle_kernel,
        in_specs=[whole(), far_spec()],
        out_specs=[whole(), whole()],
        out_shape=[
            jax.ShapeDtypeStruct((2, rows - 2, cols, 2 * out), BF),
            jax.ShapeDtypeStruct((2, 2, cols, 2 * out), F32),
        ],
        scratch_shapes=[
            pltpu.VMEM((2, out, height // 3), BF),
            pltpu.SemaphoreType.DMA((2,)),
        ],
        compiler_params=params(),
        cost_estimate=pl.CostEstimate(
            flops=2 * 2 * 2 * 3 * cols * 9 * channels * out,
            bytes_accessed=2 * (own.size + weight.size),
            transcendentals=0,
        ),
        name="middle",
    )(own, far(weight))


def edge_slices(weight_hbm, slices_ref, sems):
    depth = slices_ref.shape[3]
    return [
        pltpu.make_async_copy(
            weight_hbm.at[:, pl.ds((t * 3 + 2 * n) * depth, depth)],
            slices_ref.at[t, n],
            sems.at[t * 2 + n],
        )
        for t in range(2)
        for n in range(2)
    ]


def edge_kernel(rim_ref, above_ref, below_ref, weight_ref, out_ref, var):
    _, _, cols, channels = var.shape
    head = lax.axis_index("head")
    for n, far_rim in enumerate((above_ref, below_ref)):
        even, odd = far_rim[:cols], far_rim[cols : 2 * cols]
        var[n, 0] = shift_down(odd.astype(F32)).astype(BF)
        var[n, 1] = even
        var[n, 2] = odd
        var[n, 3] = shift_up(even.astype(F32)).astype(BF)

    def contribute(f, t):
        for n in range(2):
            late = tap_sum(lambda v, r: var[n, v], (0,), (0,), weight_ref[t, n])
            out_ref[f, n] = (rim_ref[f, n] + late).astype(BF)

    contribute(head, 0)

    @pl.when(head == 0)
    def _():
        out_ref[1] = jnp.zeros(out_ref.shape[1:], BF)

    @pl.when(head != 0)
    def _():
        contribute(0, 1)


def edges(rim, above, below, weight, channels):
    _, _, cols, width = rim.shape
    out = weight.shape[2]
    return pl.pallas_call(
        edge_kernel,
        in_specs=[whole()] * 4,
        out_specs=whole(),
        out_shape=jax.ShapeDtypeStruct(rim.shape, BF),
        scratch_shapes=[pltpu.VMEM((2, 4, cols, channels), BF)],
        compiler_params=params(),
        cost_estimate=pl.CostEstimate(
            flops=2 * 2 * 2 * 2 * cols * 3 * channels * out,
            bytes_accessed=2 * (above.size + weight.size),
            transcendentals=0,
        ),
        name="edge",
    )(rim, above, below, weight)


def mix_kernel(weight_ref, out_ref):
    channels = weight_ref.shape[1] // 9

    def tap(h, w):
        start = (h * 3 + w) * channels
        return weight_ref[:, start : start + channels]

    lines = {}
    for w in range(3):
        top, middle, bottom = tap(0, w), tap(1, w), tap(2, w)
        lines[0, 0, w] = top
        lines[0, 1, w] = middle + bottom
        lines[1, 0, w] = top + middle
        lines[1, 1, w] = bottom
    for a in range(2):
        for u in range(2):
            left, centre, right = [lines[a, u, w] for w in range(3)]
            mixed = ((left, centre + right), (left + centre, right))
            for b in range(2):
                for v in range(2):
                    start = (u * 2 + v) * channels
                    out_ref[0, a * 2 + b, :, start : start + channels] = mixed[b][v]


def mix(weight):
    out, height = weight.shape
    third = height // 3
    shape = (3, 4, out, third // 9 * 4)
    return pl.pallas_call(
        mix_kernel,
        grid=(3,),
        in_specs=[pl.BlockSpec((out, third), lambda t: (0, t))],
        out_specs=pl.BlockSpec((1,) + shape[1:], lambda t: (t, 0, 0, 0)),
        out_shape=jax.ShapeDtypeStruct(shape, BF),
        compiler_params=params(1),
        cost_estimate=pl.CostEstimate(
            flops=4 * weight.size, bytes_accessed=6 * weight.size, transcendentals=0
        ),
        name="mix",
    )(weight)


def spread(source_ref, var):
    frames, coarse = source_ref.shape[:2]
    for f in range(frames):
        for r in range(coarse):
            plain = source_ref[f, r]
            wide = plain.astype(F32)
            var[0, f, r] = shift_down(wide).astype(BF)
            var[1, f, r] = plain
            var[2, f, r] = shift_up(wide).astype(BF)


def taps(var, frames, a, b):
    coarse = var.shape[2]
    lines = []
    for frame in frames:
        for r in range(coarse - 2):
            lines.append(
                jnp.concatenate(
                    [var[b + v, frame, r + a + u] for u in range(2) for v in range(2)], axis=1
                )
            )
    return jnp.concatenate(lines, axis=0)


def own_kernel(source_ref, old_ref, new_ref, out_ref, var):
    step = pl.program_id(0)
    a = step // 2
    b = step % 2

    @pl.when(step == 0)
    def _():
        spread(source_ref, var)

    both = dot_last(taps(var, (0, 1), a, b), new_ref[0, 0])
    more = dot_last(taps(var, (0,), a, b), old_ref[0, 0])
    height = more.shape[0]
    shape = out_ref.shape[2:]
    out_ref[0, 0] = both[:height].reshape(shape)
    out_ref[0, 1] = (both[height:] + more).reshape(shape)


def own_part(activated, mixed):
    frames, coarse, cols, channels = activated.shape
    _, parities, width, depth = mixed.shape
    block = (1, 1, width, depth)
    shape = (parities, frames, coarse - 2, cols, width)
    return pl.pallas_call(
        own_kernel,
        grid=(parities,),
        in_specs=[
            pl.BlockSpec(activated.shape, lambda i: (0, 0, 0, 0)),
            pl.BlockSpec(block, lambda i: (1, i, 0, 0)),
            pl.BlockSpec(block, lambda i: (2, i, 0, 0)),
        ],
        out_specs=pl.BlockSpec((1,) + shape[1:], lambda i: (i, 0, 0, 0, 0)),
        out_shape=jax.ShapeDtypeStruct(shape, F32),
        scratch_shapes=[pltpu.VMEM((3, frames, coarse, cols, channels), BF)],
        compiler_params=params(1),
        cost_estimate=pl.CostEstimate(
            flops=2 * 3 * 2 * cols * depth * width * parities,
            bytes_accessed=2 * (activated.size + 2 * parities * width * depth),
            transcendentals=0,
        ),
        name="own_part",
    )(activated, mixed, mixed)


def prior_kernel(source_ref, middle_ref, edge_ref, own_ref, old_ref, new_ref, out_ref, var, total_ref, scr):
    parities, frames, coarse_rows, cols, width = total_ref.shape
    head = lax.axis_index("head")
    step = pl.program_id(0)
    a = step // 2
    b = step % 2

    @pl.when(head == 0)
    def _():
        total_ref[step] = own_ref[0]

    @pl.when(head != 0)
    def _():
        @pl.when(step == 0)
        def _():
            spread(source_ref, var)

        both = dot_last(taps(var, (0, 1), a, b), old_ref[0, 0])
        more = dot_last(taps(var, (1,), a, b), new_ref[0, 0])
        height = more.shape[0]
        shape = total_ref.shape[2:]
        total_ref[step, 0] = own_ref[0, 0] + (both[:height] + more).reshape(shape)
        total_ref[step, 1] = own_ref[0, 1] + both[height:].reshape(shape)

    @pl.when(step == parities - 1)
    def _():
        fine = 2 * coarse_rows
        pieces = 2 * width // 128

        def assemble(extra):
            for f in range(frames):
                for row in range(fine):
                    side = (row % 2) * 2
                    sides = [total_ref[side + n, f, row // 2] for n in range(2)]
                    line = jnp.concatenate(sides, axis=1)
                    if extra:
                        if row in (0, fine - 1):
                            mine = edge_ref[f, min(row, 1)]
                        else:
                            mine = middle_ref[f, row - 1]
                        line = line + (mine.astype(F32) + source_ref[f, row].astype(F32))
                    for q in range(pieces):
                        at = f * cols * pieces * fine + q * fine + row
                        scr[pl.ds(at, cols, stride=pieces * fine), :] = line[
                            :, q * 128 : (q + 1) * 128
                        ]
                for at in range(out_ref.shape[1]):
                    start = (f * out_ref.shape[1] + at) * fine
                    out_ref[f, at] = scr[start : start + fine, :].astype(BF)

        @pl.when(head == 0)
        def _():
            assemble(True)

        @pl.when(head != 0)
        def _():
            assemble(False)


def prior_part(received, middle, edge, own_sum, mixed):
    frames, coarse, cols, channels = received.shape
    _, parities, width, depth = mixed.shape
    fine = 2 * (coarse - 2)
    tiles = cols * 2 * width // 128
    block = (1, 1, width, depth)
    out = pl.pallas_call(
        prior_kernel,
        grid=(parities,),
        in_specs=[
            pl.BlockSpec(received.shape, lambda i: (0, 0, 0, 0)),
            pl.BlockSpec(middle.shape, lambda i: (0, 0, 0, 0)),
            pl.BlockSpec(edge.shape, lambda i: (0, 0, 0, 0)),
            pl.BlockSpec((1,) + own_sum.shape[1:], lambda i: (i, 0, 0, 0, 0)),
            pl.BlockSpec(block, lambda i: (0, i, 0, 0)),
            pl.BlockSpec(block, lambda i: (1, i, 0, 0)),
        ],
        out_specs=pl.BlockSpec((frames, tiles, fine, 128), lambda i: (0, 0, 0, 0)),
        out_shape=jax.ShapeDtypeStruct((frames, tiles, fine, 128), BF),
        scratch_shapes=[
            pltpu.VMEM((3, frames, coarse, cols, channels), BF),
            pltpu.VMEM(own_sum.shape, F32),
            pltpu.VMEM((frames * tiles * fine, 128), F32),
        ],
        compiler_params=params(1),
        cost_estimate=pl.CostEstimate(
            flops=2 * 3 * 2 * cols * depth * width * parities,
            bytes_accessed=2 * (received.size + 2 * parities * width * depth),
            transcendentals=0,
        ),
        name="prior_part",
    )(received, middle, edge, own_sum, mixed, mixed)
    return out.transpose(0, 2, 1, 3).reshape(frames, fine, tiles * 128)


def latent_kernel(
    step_ref, parts_ref, own_ref, above_ref, below_ref, weight_hbm, clean_ref, send_ref, out_ref, slices_ref, scr, sems
):
    copies = edge_slices(weight_hbm, slices_ref, sems)
    for copy in copies:
        copy.start()
    sources, three, unit, lanes = parts_ref.shape
    cols = own_ref.shape[0]
    frames, chunks, halves = out_ref.shape[:3]
    groups = frames * halves
    group = lanes // groups
    features = sources * 128
    fraction = 1.0 - step_ref[0].astype(F32) / NSTEPS
    fraction = jnp.full((1, lanes), fraction, F32)
    level = SHIFT_FACTOR * fraction / (1.0 + (SHIFT_FACTOR - 1.0) * fraction)
    total = parts_ref[0].astype(F32)
    for source in range(1, sources):
        total = total + parts_ref[source].astype(F32)
    half = lax.broadcasted_iota(jnp.int32, (cols, lanes), 1) < lanes // 2
    first_group = lax.axis_index("head") == 0
    for k, small_ref in ((0, above_ref), (1, own_ref), (2, below_ref)):
        small = small_ref[...] if k == 1 else small_ref[small_ref.shape[0] - cols :]
        sums = jnp.transpose(total[k, cols:unit])[:cols]
        scale = lax.rsqrt(sums / features + NORM_EPSILON)
        scale = jnp.where(half, scale[:, 0:1], scale[:, 1:2])
        velocity = total[k, :cols] * scale
        clean = (small[:, :lanes].astype(F32) - level * velocity).astype(BF)
        clean_ref[k] = clean
        if k == 1:
            scr[:cols, :] = clean.astype(F32)

        @pl.when(first_group)
        def _():
            send_ref[k] = clean

        @pl.when(jnp.logical_not(first_group))
        def _():
            send_ref[k] = small[:, lanes : 2 * lanes]

    parts = [scr[pl.ds(m, chunks, stride=groups), :] for m in range(groups)]
    for g in range(groups):
        total_line = None
        for m, part in enumerate(parts):
            term = jnp.where(lane_groups(part, group) == m, moved(part, group * (m - g)), 0.0)
            total_line = term if total_line is None else total_line + term
        f, a = g // halves, g % halves
        scr[pl.ds(cols + f * chunks * halves + a, chunks, stride=halves), :] = total_line
    for f in range(frames):
        for i in range(chunks):
            at = cols + (f * chunks + i) * halves
            out_ref[f, i] = scr[at : at + halves, :].astype(BF)
    for copy in copies:
        copy.wait()


def latent(step_index, parts, own, above, below, weight, frames, halves, chunks):
    sources, three, unit, lanes = parts.shape
    cols = own.shape[0]
    shape = jax.ShapeDtypeStruct((three, cols, lanes), BF)
    return pl.pallas_call(
        latent_kernel,
        in_specs=[smem()] + [whole()] * 4 + [far_spec()],
        out_specs=[whole()] * 4,
        out_shape=[
            shape,
            shape,
            jax.ShapeDtypeStruct((frames, chunks, halves, 128), BF),
            jax.ShapeDtypeStruct((2, 2, weight.shape[0], weight.shape[1] // 9), BF),
        ],
        scratch_shapes=[
            pltpu.VMEM((cols + frames * chunks * halves, lanes), F32),
            pltpu.SemaphoreType.DMA((4,)),
        ],
        compiler_params=params(0, 8),
        cost_estimate=pl.CostEstimate(
            flops=2 * parts.size, bytes_accessed=2 * parts.size, transcendentals=0
        ),
        name="latent",
    )(step_index, parts, own, above, below, far(weight))


def first_kernel(
    clean_ref, received_ref, own_ref, above_ref, below_ref, weight_ref, gain_ref, middle_ref, edge_ref, act_ref, send_ref, left, padded, scr
):
    three, cols, lanes = clean_ref.shape
    frames, coarse = act_ref.shape[:2]
    channels = act_ref.shape[3]
    group = lanes // 4
    slot = lanes // 2
    part = group // 2
    head = lax.axis_index("head")
    three_taps = weight_ref.shape[0] // 9
    gap = jnp.zeros((slot - three_taps, channels), BF)
    for n in range(9):
        padded[n * slot : n * slot + three_taps, :] = weight_ref[
            n * three_taps : (n + 1) * three_taps, :
        ]
        padded[n * slot + three_taps : (n + 1) * slot, :] = gap
    padded[9 * slot :, :] = jnp.zeros((slot, channels), BF)
    gains = gain_ref[...].astype(F32)
    gain = jnp.concatenate([gains[q : q + 1] for q in range(gains.shape[0])], axis=1)
    cached_old = jnp.concatenate(
        [
            above_ref[above_ref.shape[0] - cols :, lanes : 2 * lanes].astype(F32),
            own_ref[:, lanes : 2 * lanes].astype(F32),
            below_ref[below_ref.shape[0] - cols :, lanes : 2 * lanes].astype(F32),
        ],
        axis=0,
    )
    clean = jnp.concatenate([clean_ref[k].astype(F32) for k in range(three)], axis=0)
    arrived = jnp.concatenate([received_ref[k].astype(F32) for k in range(three)], axis=0)
    lane = lax.broadcasted_iota(jnp.int32, clean.shape, 1)
    line = lax.broadcasted_iota(jnp.int32, clean.shape, 0)
    at = lax.rem(line, cols)
    older = jnp.where(
        head == 0, jnp.where(lane < lanes // 2, cached_old, arrived), arrived
    )
    pieces = {}
    for source, x in enumerate((older, clean)):
        height = x.shape[0]
        before = jnp.where(at == 0, 0.0, pltpu.roll(x, 1, axis=0))
        after = jnp.where(at == cols - 1, 0.0, pltpu.roll(x, height - 1, axis=0))
        for f in range(2):
            for a in range(2):
                off = f * (lanes // 2) + a * group
                for side in range(2):
                    base = side * slot

                    low = lane - base
                    even = jnp.where(
                        (low >= 0) & (low < part),
                        moved(before, base - off - part),
                        jnp.where(
                            (low >= part) & (low < 3 * part), moved(x, base + part - off), 0.0
                        ),
                    )
                    odd = jnp.where(
                        (low >= 0) & (low < 2 * part),
                        moved(x, base - off),
                        jnp.where(
                            (low >= 2 * part) & (low < 3 * part),
                            moved(after, base + 2 * part - off),
                            0.0,
                        ),
                    )
                    pieces[source * 2 + f, a, side, 0] = even
                    pieces[source * 2 + f, a, side, 1] = odd

    def piece(p, fo, ro, n):
        frame = fo + n // 3
        row = ro + n % 3
        k = row // 2
        return pieces[frame, row % 2, n % 2, p][k * cols : (k + 1) * cols]

    for p in range(2):
        for fo in range(frames):
            for ro in range(coarse):
                start = ((p * frames + fo) * coarse + ro) * cols
                for j in range(5):
                    block = piece(p, fo, ro, 2 * j)
                    if 2 * j + 1 < 9:
                        block = block + piece(p, fo, ro, 2 * j + 1)
                    left[start : start + cols, j * lanes : (j + 1) * lanes] = block.astype(BF)

    feat = dot(left[...], padded[...])
    mean_square = jnp.mean(feat * feat, axis=-1, keepdims=True)
    normed = feat * lax.rsqrt(mean_square + NORM_EPSILON) * gain
    active = normed / (1.0 + jnp.exp(-normed))
    slab = lax.axis_index("seq")
    last = lax.axis_size("seq") - 1
    keep_first = jnp.where(slab == 0, 0.0, 1.0)
    keep_last = jnp.where(slab == last, 0.0, 1.0)
    for p in range(2):
        for fo in range(frames):
            for ro in range(coarse):
                start = ((p * frames + fo) * coarse + ro) * cols
                block = active[start : start + cols]
                if ro == 0:
                    block = block * keep_first
                if ro == coarse - 1:
                    block = block * keep_last
                to = (fo * coarse + ro) * 2 * cols + p
                for q in range(channels // 128):
                    scr[q, pl.ds(to, cols, stride=2), :] = block[:, q * 128 : (q + 1) * 128]
    for fo in range(frames):
        for ro in range(coarse):
            to = (fo * coarse + ro) * 2 * cols
            for q in range(channels // 128):
                act_ref[fo, ro, :, q * 128 : (q + 1) * 128] = scr[q, to : to + 2 * cols, :].astype(BF)

    @pl.when(head == 0)
    def _():
        send_ref[...] = act_ref[...]

    @pl.when(head != 0)
    def _():
        for fo in range(frames):
            send_ref[fo, 0] = edge_ref[fo, 0]
            send_ref[fo, coarse - 1] = edge_ref[fo, 1]
            for ro in range(1, coarse - 1):
                send_ref[fo, ro] = middle_ref[fo, ro - 1]


def first(clean, received, own, above, below, weight, gain, middle, edge):
    three, cols, lanes = clean.shape
    frames, inner, wide, channels = middle.shape
    coarse = inner + 2
    shape = jax.ShapeDtypeStruct((frames, coarse, wide, channels), BF)
    height = frames * coarse * wide
    return pl.pallas_call(
        first_kernel,
        in_specs=[whole()] * 9,
        out_specs=[whole(), whole()],
        out_shape=[shape, shape],
        scratch_shapes=[
            pltpu.VMEM((height, 5 * lanes), BF),
            pltpu.VMEM((5 * lanes, channels), BF),
            pltpu.VMEM((channels // 128, height, 128), F32),
        ],
        compiler_params=params(),
        cost_estimate=pl.CostEstimate(
            flops=2 * height * weight.size, bytes_accessed=8 * middle.size, transcendentals=height * channels
        ),
        name="first",
    )(clean, received, own, above, below, weight, gain, middle, edge)


def swapped(array, axis):
    return lax.ppermute(array, axis, [(0, 1), (1, 0)])


def body(
    queries,
    keys,
    values,
    final_gain,
    out_weight,
    noisy_latent,
    step_index,
    span_index,
    cache_flags,
    latent_cache,
    feature_cache,
    first_weight,
    first_gain,
    second_weight,
):
    channels = first_weight.shape[1]
    slabs = lax.axis_size("seq")
    frames, halves, width = noisy_latent.shape
    second = second_weight.T

    sent, facts, cache, noisy, latents = attention(
        queries,
        keys,
        values,
        final_gain,
        out_weight,
        cache_flags,
        feature_cache,
        noisy_latent,
        latent_cache,
    )
    parts = lax.all_to_all(sent, "seq", 0, 0, tiled=True)
    own_frame, up, down, small = prepare(
        span_index, facts, cache, noisy, latents, channels
    )
    above = lax.ppermute(down, "seq", [(i, i + 1) for i in range(slabs - 1)])
    below = lax.ppermute(up, "seq", [(i + 1, i) for i in range(slabs - 1)])
    middle, rim = middles(own_frame, second)
    above, below, middle = lax.optimization_barrier((above, below, middle))

    clean, send, out, slices = latent(
        step_index, parts, small, above, below, second, frames, halves, width // 128
    )
    edge = edges(rim, above, below, slices, channels)
    received = swapped(send, "head")
    activated, send = first(
        clean, received, small, above, below, first_weight, first_gain.reshape(-1, 128), middle, edge
    )
    arrived = swapped(send, "head")
    mixed = mix(second)
    own_sum = own_part(activated, mixed)
    decoded = prior_part(arrived, middle, edge, own_sum, mixed)
    return (out.transpose(0, 2, 1, 3).reshape(frames, halves, width), decoded)


def solution(mesh):
    in_specs = (
        P(("grp", "head"), None, None, "seq"),
        P("grp", None, None, "seq"),
        P("grp", None, None, "seq"),
        P(),
        P(),
        P(("grp", "head"), "seq", None),
        P("grp"),
        P("grp"),
        P("grp", None, None),
        P("grp", "head", "seq", None),
        P("grp", "head", "seq", None),
        P(),
        P(),
        P(),
    )
    out_specs = (P(("grp", "head"), "seq", None), P(("grp", "head"), "seq", None))
    return jax.shard_map(body, mesh=mesh, in_specs=in_specs, out_specs=out_specs, check_vma=False)
```
